32 devices in a mesh: strip: 8 (over z, x), seq: 4 (over y, core).
Axes of the slice: x: 2, y: 2, z: 4, core: 2. Of those that a mesh axis runs over, the one named last changes fastest.
Arguments:
- slide_image: bfloat16 [3, 256, 4096], P(None, 'strip', 'seq'), may hold values from -6 to 6
- keep_flags: int32 [16, 256], P('strip', 'seq'), may hold values from 0 to 1, as said below
- owner_shift: int32 [4], P('seq'), may hold values from 0 to 7
- weight_one: bfloat16 [9, 64, 3], replicated, may hold values from -1.25 to 1.25
- offset_one: float32 [64], replicated, may hold values from -3 to 3
- weight_two: bfloat16 [9, 128, 64], replicated, may hold values from -0.25 to 0.25
- offset_two: float32 [128], replicated, may hold values from -3 to 3
- weight_three: bfloat16 [9, 256, 128], replicated, may hold values from -0.1875 to 0.1875
- offset_three: float32 [256], replicated, may hold values from -3 to 3
- patch_weight: bfloat16 [4, 256, 1536], replicated, may hold values from -0.1875 to 0.1875
- patch_offset: float32 [1536], replicated, may hold values from -3 to 3
Outputs:
- sequences: bfloat16 [4, 512, 1536], P('seq', 'strip')
The draws below stay inside these ranges and needn't reach their ends.
Inputs may be any that keep to these rules, and one draw needn't show every extreme that they name: `keep_flags`: exactly half of the patches of each band are kept; some device of each band keeps all 128 of its patches and another keeps none.
All inputs are finite; a program needn't handle non-finite values.
Results may differ from the reference program's by a relative error of at most 0.0049.
Values may be sent and summed in bfloat16 or wider, within the bound.
A program may use at most 128 MiB of HBM per device.

```python
import jax
import jax.numpy as jnp
from jax import lax

STEM_ONE = 64
STEM_TWO = 128
STEM_THREE = 256
EMBED = 1536
ROWS_DEV = 32
PATCH_ROWS_DEV = 2
PATCH_COLS_DEV = 64
PATCH_DEV = 128
OWN_DEV = 64
IMG_ROWS = 256
IMG_COLS = 4096
PATCH_ROWS = 16
SEQS = 4
SEQ_LEN = 512
N_STRIP = 8
N_SEQ = 4


def draw_keep_flags(key, part):
    pair_key, force_key, place_key, perm_key = jax.random.split(key, 4)
    pair_count = N_STRIP // 2
    share_one = jax.random.randint(pair_key, (N_SEQ, pair_count), 0, PATCH_DEV + 1)
    forced = jax.random.randint(force_key, (N_SEQ,), 0, pair_count)
    share_one = jnp.where(jnp.arange(pair_count)[None, :] == forced[:, None], PATCH_DEV, share_one)
    paired = jnp.stack([share_one, PATCH_DEV - share_one], axis=2).reshape(N_SEQ, N_STRIP)
    place_keys = jax.random.split(place_key, N_SEQ)

    def one_shuffle(subkey):
        return jax.random.permutation(subkey, N_STRIP).astype(jnp.int32)
    device_order = jax.vmap(one_shuffle)(place_keys)
    counts = jnp.take_along_axis(paired, device_order, axis=1)
    perm_keys = jax.random.split(perm_key, N_SEQ * N_STRIP)

    def one_order(subkey):
        return jax.random.permutation(subkey, PATCH_DEV)
    rank_table = jax.vmap(one_order)(perm_keys).reshape(N_SEQ, N_STRIP, PATCH_ROWS_DEV, PATCH_COLS_DEV)
    keep_table = (rank_table < counts[:, :, None, None]).astype(jnp.int32)
    return keep_table.transpose(1, 2, 0, 3).reshape(N_STRIP * PATCH_ROWS_DEV, N_SEQ * PATCH_COLS_DEV)


def touch_ends(values, own_key, low, largest):
    spot = [jax.random.randint(jax.random.fold_in(own_key, axis), (), 0, length) for axis, length in enumerate(values.shape)]
    longest = values.shape.index(max(values.shape))
    beside = spot[:longest] + [(spot[longest] + 1) % values.shape[longest]] + spot[longest + 1:]
    return values.at[tuple(spot)].set(low).at[tuple(beside)].set(largest)


def level_of(own_key, shape, cuts, low, top_value):
    level = 1.0
    for axis_at, shards_of in cuts:
        heights = jax.random.uniform(jax.random.fold_in(jax.random.fold_in(own_key, 6), axis_at), (shards_of,), jnp.float32, low / len(cuts), top_value / len(cuts))
        level = level * jnp.repeat(jnp.exp(heights), shape[axis_at] // shards_of).reshape((-1,) + (1,) * (len(shape) - 1 - axis_at))
    return level


def bell_draw(rng, extent, deviation, bound, cuts=(), held_as=jnp.bfloat16):
    factor_of = level_of(rng, extent, cuts, -0.22, 0.18) if cuts else 1.0
    array = jax.random.normal(rng, extent, jnp.float32) * deviation * factor_of
    return jnp.minimum(jnp.maximum(array, -bound), bound).astype(held_as)


def setup_inputs(seed: int = 0) -> dict:
    seeds = jax.random.split(jax.random.key(seed), 12)
    slide_image = bell_draw(seeds[0], (3, IMG_ROWS, IMG_COLS), 1.0, 6.0, ((1, 8), (2, 4)))
    keep_flags = draw_keep_flags(jax.random.fold_in(seeds[11], 71), 0)
    owner_shift = touch_ends(jax.random.randint(seeds[2], (SEQS,), 0, N_STRIP), jax.random.fold_in(seeds[2], 1), 0, N_STRIP - 1).astype(jnp.int32)
    weight_one = bell_draw(seeds[3], (9, STEM_ONE, 3), 27 ** -0.5, 1.25)
    offset_one = bell_draw(seeds[4], (STEM_ONE,), 0.5, 3.0, (), jnp.float32)
    weight_two = bell_draw(seeds[5], (9, STEM_TWO, STEM_ONE), (9 * STEM_ONE) ** -0.5, 0.25)
    offset_two = bell_draw(seeds[6], (STEM_TWO,), 0.5, 3.0, (), jnp.float32)
    weight_three = bell_draw(seeds[7], (9, STEM_THREE, STEM_TWO), (9 * STEM_TWO) ** -0.5, 0.1875)
    offset_three = bell_draw(seeds[8], (STEM_THREE,), 0.5, 3.0, (), jnp.float32)
    patch_weight = bell_draw(seeds[9], (4, STEM_THREE, EMBED), (4 * STEM_THREE) ** -0.5, 0.1875)
    patch_offset = bell_draw(seeds[10], (EMBED,), 0.5, 3.0, (), jnp.float32)
    return {"slide_image": slide_image, "keep_flags": keep_flags, "owner_shift": owner_shift, "weight_one": weight_one, "offset_one": offset_one, "weight_two": weight_two, "offset_two": offset_two, "weight_three": weight_three, "offset_three": offset_three, "patch_weight": patch_weight, "patch_offset": patch_offset}


def convolve(padded, weights, offsets):
    channels = padded.shape[0]
    rows_out = (padded.shape[1] - 1) // 2
    cols_out = (padded.shape[2] - 1) // 2
    summed = jnp.zeros((weights.shape[1], rows_out, cols_out), jnp.float32)
    for row_tap in range(3):
        for col_tap in range(3):
            window = lax.slice(padded, (0, row_tap, col_tap), (channels, row_tap + 2 * rows_out - 1, col_tap + 2 * cols_out - 1), (1, 2, 2))
            summed = summed + jnp.einsum("oc,crw->orw", weights[3 * row_tap + col_tap].astype(jnp.float32), window.astype(jnp.float32))
    return jax.nn.gelu(summed + offsets[:, None, None], approximate=False).astype(jnp.bfloat16)


def reference(slide_image, keep_flags, owner_shift, weight_one, offset_one, weight_two, offset_two, weight_three, offset_three, patch_weight, patch_offset):
    layers = ((weight_one, offset_one), (weight_two, offset_two), (weight_three, offset_three))
    strip_blocks = slide_image.reshape(3, N_STRIP, ROWS_DEV, IMG_COLS).transpose(1, 0, 2, 3)

    def strip_step(upper_rows, strip_block):
        new_rows = []
        feature_map = strip_block
        for layer_index in range(3):
            weights, offsets = layers[layer_index]
            tall_block = jnp.concatenate([upper_rows[layer_index], feature_map], axis=1)
            padded = jnp.pad(tall_block, ((0, 0), (0, 0), (1, 0)))
            new_rows.append(feature_map[:, -1:, :])
            feature_map = convolve(padded, weights, offsets)
        summed = jnp.zeros((feature_map.shape[1] // 2, feature_map.shape[2] // 2, EMBED), jnp.float32)
        for row_half in range(2):
            for col_half in range(2):
                quarter = feature_map[:, row_half::2, col_half::2].astype(jnp.float32)
                summed = summed + jnp.einsum("cpq,ce->pqe", quarter, patch_weight[2 * row_half + col_half].astype(jnp.float32))
        tokens = (summed + patch_offset).astype(jnp.bfloat16)
        return tuple(new_rows), tokens

    start_rows = (jnp.zeros((3, 1, IMG_COLS), jnp.bfloat16), jnp.zeros((STEM_ONE, 1, IMG_COLS // 2), jnp.bfloat16), jnp.zeros((STEM_TWO, 1, IMG_COLS // 4), jnp.bfloat16))
    _, tokens = lax.scan(strip_step, start_rows, strip_blocks)
    tokens = tokens.reshape(PATCH_ROWS, SEQS, PATCH_COLS_DEV, EMBED).transpose(1, 0, 2, 3).reshape(SEQS, PATCH_ROWS * PATCH_COLS_DEV, EMBED)
    band_flags = keep_flags.reshape(PATCH_ROWS, SEQS, PATCH_COLS_DEV).transpose(1, 0, 2).reshape(SEQS, PATCH_ROWS * PATCH_COLS_DEV)
    position = (jnp.cumsum(band_flags, axis=1, dtype=jnp.int32) - band_flags).astype(jnp.int32)
    owner_index = (position + owner_shift[:, None].astype(jnp.int32)) % N_STRIP
    target = jnp.where(band_flags == 1, owner_index * OWN_DEV + position // N_STRIP, SEQ_LEN).astype(jnp.int32)

    def place(row_ids, band_tokens):
        return jnp.zeros((SEQ_LEN, EMBED), jnp.bfloat16).at[row_ids].set(band_tokens, mode="drop")

    return jax.vmap(place)(target, tokens)
```

```python
import functools

import jax
import jax.numpy as jnp
from jax import lax
from jax.experimental import pallas as pl
from jax.experimental.pallas import tpu as pltpu
from jax.sharding import PartitionSpec as P

MESH = pl.DeviceIdType.MESH
F32 = jnp.float32
BF16 = jnp.bfloat16

M1 = 560
M2 = 272
M3 = 128
VMEM1 = 60000000


def gelu(x):
    return 0.5 * x * (1.0 + lax.erf(x * 0.7071067811865476))


def dot(a, b):
    return jnp.dot(a, b, preferred_element_type=F32)


def dot_nt(a, b):
    return lax.dot_general(a, b, (((1,), (1,)), ((), ())), preferred_element_type=F32)


def kernel(
    n, n_seq, cap,
    shift_ref, img_hbm, flag_hbm, w1_hbm, b1_hbm, w2_hbm, b2_hbm, w3_hbm, b3_hbm, pw_hbm,
    out_ref, pw_out,
    img_ref, flag_ref, w1_ref, b1_ref, w2_ref, b2_ref, w3_ref, b3_ref, top, left, corner, flags, band, slab, slab_t, a1, k1, s1, s2, s3, sendbuf, got,
    halo_send, halo_recv, flag_send, flag_recv, row_send, row_recv, load_sem, pw_sem,
):
    me = lax.axis_index("strip")
    mq = lax.axis_index("seq")
    half = n // 2
    late = me // half
    down, up = lax.rem(me + 1, n), lax.rem(me + n - 1, n)
    right, leftward = lax.rem(mq + 1, n_seq), lax.rem(mq + n_seq - 1, n_seq)

    loads = [
        pltpu.make_async_copy(src, dst, load_sem.at[k])
        for k, (src, dst) in enumerate(
            (
                (w1_hbm, w1_ref), (img_hbm, img_ref), (b1_hbm, b1_ref), (w2_hbm, w2_ref),
                (b2_hbm, b2_ref), (w3_hbm, w3_ref), (b3_hbm, b3_ref), (flag_hbm, flag_ref),
            )
        )
    ]
    barrier = pltpu.get_barrier_semaphore()

    def greet(i, c):
        pl.semaphore_signal(barrier, inc=1, device_id=(lax.rem(me + i, n), mq), device_id_type=MESH)
        return c

    for load in loads[:2]:
        load.start()
    for where in ((me, right), (me, leftward), (down, right), (up, leftward)):
        pl.semaphore_signal(barrier, inc=1, device_id=where, device_id_type=MESH)
    lax.fori_loop(1, n, greet, 0)
    for load in loads[2:]:
        load.start()

    pw_copy = pltpu.make_async_copy(pw_hbm, pw_out, pw_sem)

    def flag_copy(i, source):
        return pltpu.make_async_remote_copy(
            src_ref=flag_hbm, dst_ref=flags.at[source],
            send_sem=flag_send.at[i], recv_sem=flag_recv.at[i],
            device_id=(lax.rem(me + i, n), mq), device_id_type=MESH,
        )

    halos = [
        pltpu.make_async_remote_copy(
            src_ref=src, dst_ref=dst, send_sem=halo_send.at[k], recv_sem=halo_recv.at[k],
            device_id=where, device_id_type=MESH,
        )
        for k, (src, dst, where) in enumerate(
            (
                (img_ref.at[:, 24:32, :], top, (down, mq)),
                (img_ref.at[:, :, 896:1024], left, (me, right)),
                (img_ref.at[:, 24:32, 896:1024], corner, (down, right)),
            )
        )
    ]
    inner_row = me > 0
    inner_col = mq > 0
    to_down, to_right = me < n - 1, mq < n_seq - 1
    sends = (to_down, to_right, jnp.logical_and(to_down, to_right))
    receives = (inner_row, inner_col, jnp.logical_and(inner_row, inner_col))

    def send_flags(i, c):
        flag_copy(i, me).start()
        return c

    def enter():
        pl.semaphore_wait(barrier, n - 1 + 4)
        for halo, sent in zip(halos, sends):
            pl.when(sent)(halo.start)
        lax.fori_loop(1, n, send_flags, 0)

    loads[0].wait()
    low = lax.broadcasted_iota(jnp.int32, (8, 128), 0)
    low_lane = lax.broadcasted_iota(jnp.int32, (8, 128), 1)
    tap = low - 1 - 2 * jnp.where(low_lane >= 64, 1, 0)
    band[...] = jnp.zeros_like(band)
    for dx in range(3):
        tap_w = [w1_ref[3 * dy + dx].astype(F32) for dy in range(3)]
        tap_w = [jnp.concatenate([w, w], axis=1) for w in tap_w]
        for c in range(3):
            block = jnp.zeros((8, 128), F32)
            for dy in range(3):
                block = jnp.where(tap == dy, jnp.broadcast_to(tap_w[dy][c : c + 1], (8, 128)), block)
            band[dx, c, 40:48, :] = block
        for q in range(10):
            parts = [band[dx, c, 40 - 4 * q : 80 - 4 * q, :] for c in range(3)]
            parts = jnp.concatenate(parts + [jnp.zeros((8, 128), F32)], axis=0)
            k1[128 * dx : 128 * dx + 128, 128 * q : 128 * q + 128] = parts.astype(BF16)

    slab[120:128, :] = jnp.zeros((8, 1152), F32)
    slab[:120, 0:128] = jnp.zeros((120, 128), F32)
    loads[1].wait()
    for c in range(3):
        slab[40 * c : 40 * c + 8, 128:1152] = jnp.zeros((8, 1024), F32)
        slab[40 * c + 8 : 40 * c + 40, 128:1152] = img_ref[c].astype(F32)
    slab_t[1152:1280, :] = jnp.zeros((128, 128), F32)

    def fill_a1():
        for t in range(9):
            slab_t[128 * t : 128 * t + 128, :] = slab[:, 128 * t : 128 * t + 128].T
        for dx in range(3):
            a1[:, 128 * dx : 128 * dx + 128] = slab_t[pl.ds(119 + dx, M1, stride=2), :].astype(BF16)

    fill_a1()
    loads[2].wait()
    b1 = jnp.concatenate([b1_ref[...]] * 4, axis=1)

    def layer_one(t, rows):
        act = gelu(dot(a1[:rows], k1[:, 256 * t : 256 * t + 256]) + b1)
        if t == 0 or rows < M1:
            sub1 = lax.broadcasted_iota(jnp.int32, (rows, 256), 0)
            ok = jnp.logical_or(inner_col, sub1 >= 4)
            if t == 0:
                lane1 = lax.broadcasted_iota(jnp.int32, (rows, 256), 1)
                ok = jnp.logical_and(ok, jnp.logical_or(inner_row, lane1 >= 192))
            act = jnp.where(ok, act, 0.0)
        s1[2 * t, :rows] = act[:, :128]
        s1[2 * t + 1, :rows] = act[:, 128:]

    def layer_two(where, rows):
        summed = None
        for dx in range(3):
            a = jnp.concatenate(
                [
                    jnp.concatenate(
                        [s1[r + h, pl.ds(1 + dx, rows, stride=2), :] for r in where], axis=0
                    ).astype(BF16)
                    for h in range(2)
                ],
                axis=1,
            )
            w2 = jnp.concatenate(
                [w2_ref[dx], w2_ref[3 + dx], w2_ref[6 + dx], jnp.zeros((64, 128), BF16)], axis=0
            )
            part = dot(a, w2)
            summed = part if summed is None else summed + part
        act = gelu(summed + b2_ref[...])
        sub2 = lax.broadcasted_iota(jnp.int32, (rows, 128), 0)
        col_ok2 = jnp.logical_or(inner_col, sub2 >= 1)
        for k, r in enumerate(where):
            one = act[rows * k : rows * k + rows]
            if r < 2 or rows < M2:
                ok = jnp.logical_and(col_ok2, inner_row) if r == 0 else col_ok2
                one = jnp.where(ok, one, 0.0)
            s2[r, :rows] = one

    def layer_three(where, rows):
        summed = None
        for dy in range(3):
            for dx in range(3):
                a = jnp.concatenate(
                    [s2[2 * r + dy, pl.ds(dx, rows, stride=2), :] for r in where], axis=0
                ).astype(BF16)
                part = dot_nt(a, w3_ref[3 * dy + dx])
                summed = part if summed is None else summed + part
        act = gelu(summed + b3_ref[...])
        for k, r in enumerate(where):
            s3[0, r, :rows] = act[rows * k : rows * k + rows, :128]
            s3[1, r, :rows] = act[rows * k : rows * k + rows, 128:]

    for t in range(1, 5):
        layer_one(t, M1)
    pl.when(late == 1)(enter)
    for load in loads[3:]:
        load.wait()
    pw_copy.start()
    for r in range(4, 9):
        layer_two([r], M2)
    for r in (2, 3):
        layer_three([r], M3)
    pl.when(late == 0)(enter)
    for r in (2, 3):
        layer_two([r], M2)
    layer_three([1], M3)

    for buf, received, halo in zip((top, left, corner), receives, halos):
        pl.when(received)(halo.wait_recv)

        @pl.when(jnp.logical_not(received))
        def _(buf=buf):
            buf[...] = jnp.zeros_like(buf)

    for c in range(3):
        slab[40 * c : 40 * c + 8, 128:1152] = top[c].astype(F32)
        slab[40 * c + 8 : 40 * c + 40, 0:128] = left[c].astype(F32)
        slab[40 * c : 40 * c + 8, 0:128] = corner[c].astype(F32)
    fill_a1()

    flags[me] = flag_ref[...]
    own = out_ref.shape[0]
    places = n * cap
    bits = n.bit_length() - 1
    cap_bits = cap.bit_length() - 1
    shift = shift_ref[0]

    def near_flags(i, c):
        source = lax.rem(me + n - i, n)
        flag_copy(i, source).wait()
        return c + flags[source]

    def far_flags(i, c):
        flag_copy(i, lax.rem(me + n - i, n)).wait()
        return c

    def row_copy(pr, i, source):
        return pltpu.make_async_remote_copy(
            src_ref=sendbuf.at[pr, lax.rem(me + i, n)], dst_ref=got.at[pr, source],
            send_sem=row_send.at[pr, i], recv_sem=row_recv.at[pr, i],
            device_id=(lax.rem(me + i, n), mq), device_id_type=MESH,
        )

    def deal(pr, first):
        spot = lax.broadcasted_iota(jnp.int32, (places, 1), 0)
        upper = jnp.where(
            lax.broadcasted_iota(jnp.int32, (64, 64), 0) < lax.broadcasted_iota(jnp.int32, (64, 64), 1),
            1.0, 0.0,
        ).astype(BF16)
        row = flag_ref[pr : pr + 1].astype(F32)
        within = dot(jnp.broadcast_to(row, (16, 64)).astype(BF16), upper)[0:1]
        rank = jnp.where(row > 0.5, within, -1.0).astype(jnp.int32)
        wanted = (((spot >> cap_bits) - shift - first) & (n - 1)) + n * (spot & (cap - 1))
        pick = jnp.where(rank == wanted, 1.0, 0.0).astype(BF16)
        features = jnp.concatenate(
            [
                s3[h, 2 * pr + a, pl.ds(b, 64, stride=2), :].astype(BF16)
                for a in range(2) for b in range(2) for h in range(2)
            ],
            axis=1,
        )
        rows = dot(pick, features)
        sendbuf[pr] = rows.reshape(n, cap, rows.shape[1]).astype(BF16)

        def send_rows(i, c):
            row_copy(pr, i, me).start()
            return c

        lax.fori_loop(1, n, send_rows, 0)
        got[pr, me] = sendbuf[pr, me]

    for t in range(1, 5):
        layer_one(t, 16)
    layer_two(list(range(4, 9)), 8)
    layer_three([2, 3], 8)
    near = lax.fori_loop(
        1 + late * me, me + 1 + late * (n - me - 1), near_flags, jnp.zeros(flag_ref.shape, jnp.int32)
    )
    near = jnp.sum(near.astype(F32))
    mine = [jnp.sum(flag_ref[pr : pr + 1].astype(F32), axis=1, keepdims=True) for pr in range(2)]
    start = jnp.where(late == 1, n * own - near - mine[0] - mine[1], near + jnp.zeros((1, 1), F32))
    deal(1, (start + mine[0]).astype(jnp.int32))

    layer_one(0, M1)
    layer_two([0], M2)
    layer_two([1], M2)
    layer_two([2, 3], 8)
    layer_three([0], M3)
    layer_three([1], 8)
    deal(0, start.astype(jnp.int32))

    lax.fori_loop(me + 1 - late * me, n - late * (n - me - 1), far_flags, 0)
    src_of = lax.broadcasted_iota(jnp.int32, (n, places), 1) >> cap_bits
    src_at = lax.broadcasted_iota(jnp.int32, (n, places), 0)
    same = jnp.where(src_at == src_of, 1.0, 0.0).astype(BF16)
    earlier = jnp.where(src_at < src_of, 1.0, 0.0).astype(BF16)
    turn = lax.broadcasted_iota(jnp.int32, (1, places), 1) & (cap - 1)
    slots = lax.broadcasted_iota(jnp.int32, (own, places), 0)
    counts = [
        dot_nt(jnp.ones((8, 64), BF16), flags[:, pr, :].astype(F32).astype(BF16)).astype(BF16)
        for pr in range(2)
    ]
    count_l = [dot(part, same)[0:1].astype(jnp.int32) for part in counts]
    start_l = dot(counts[0], earlier)[0:1] + dot(counts[1], earlier)[0:1]
    start_l = start_l.astype(jnp.int32)
    place = []
    for pr in range(2):
        rank_l = ((me - shift - start_l) & (n - 1)) + n * turn
        slot_l = jnp.where(rank_l < count_l[pr], (start_l + rank_l) >> bits, -1)
        place.append(jnp.where(slots == slot_l, 1.0, 0.0).astype(BF16))
        start_l = start_l + count_l[pr]
    filled = jnp.sum(place[0].astype(F32), axis=1, keepdims=True)
    filled = filled + jnp.sum(place[1].astype(F32), axis=1, keepdims=True)
    width = got.shape[3]
    out_ref[:, width:] = jnp.broadcast_to(filled, (own, 128)).astype(BF16)

    placed = None
    for pr in (1, 0):

        def wait_rows(i, c, pr=pr):
            row_copy(pr, i, lax.rem(me + n - i, n)).wait()
            return c

        lax.fori_loop(1, n, wait_rows, 0)
        rows = got[pr].astype(F32).reshape(places, width).astype(BF16)
        part = dot(place[pr], rows)
        placed = part if placed is None else placed + part
    out_ref[:, :width] = placed.astype(BF16)
    for halo, sent in zip(halos, sends):
        pl.when(sent)(halo.wait_send)
    pw_copy.wait()


def project(dealt_ref, pw_ref, pb_ref, out_ref):
    width = pw_ref.shape[0] * pw_ref.shape[1]
    filled = dealt_ref[:, width:].astype(F32)
    filled = jnp.concatenate([filled, filled], axis=1)
    for t in range(6):
        cut = slice(256 * t, 256 * t + 256)
        summed = None
        for k in range(4):
            part = dot(dealt_ref[:, 256 * k : 256 * k + 256], pw_ref[k, :, cut])
            summed = part if summed is None else summed + part
        bias = jnp.concatenate([pb_ref[2 * t : 2 * t + 1], pb_ref[2 * t + 1 : 2 * t + 2]], axis=1)
        out_ref[:, cut] = jnp.where(filled > 0.5, summed + bias, 0.0).astype(BF16)


def local(n, n_seq, slide_image, keep_flags, owner_shift, weight_one, offset_one, weight_two,
          offset_two, weight_three, offset_three, patch_weight, patch_offset):
    patches = keep_flags.size
    embed = patch_weight.shape[2]
    cap = 8 * -(-(-(-keep_flags.shape[1] // n)) // 8)
    width = patch_weight.shape[0] * patch_weight.shape[1]
    arrays = (
        slide_image, keep_flags, weight_one.transpose(0, 2, 1), offset_one[None],
        weight_two.transpose(0, 2, 1), offset_two[None], weight_three, offset_three[None],
    )
    own = patches // 2
    vmem = pl.BlockSpec(memory_space=pltpu.VMEM)
    anywhere = pl.BlockSpec(memory_space=pltpu.HBM)
    dma = pltpu.SemaphoreType.DMA
    dealt, pw = pl.pallas_call(
        functools.partial(kernel, n, n_seq, cap),
        name="stem_and_deal",
        out_shape=(
            pltpu.VMEM((own, width + 128), BF16),
            pltpu.VMEM(patch_weight.shape, BF16),
        ),
        in_specs=[pl.BlockSpec(memory_space=pltpu.SMEM)] + [anywhere] * 9,
        out_specs=(vmem, pl.BlockSpec(memory_space=pltpu.VMEM)),
        scratch_shapes=[
            *(pltpu.VMEM(x.shape, x.dtype) for x in arrays),
            pltpu.VMEM((3, 8, 1024), BF16),
            pltpu.VMEM((3, 32, 128), BF16),
            pltpu.VMEM((3, 8, 128), BF16),
            pltpu.VMEM((n,) + keep_flags.shape, jnp.int32),
            pltpu.VMEM((3, 3, 80, 128), F32),
            pltpu.VMEM((128, 1152), F32),
            pltpu.VMEM((1280, 128), F32),
            pltpu.VMEM((M1, 384), BF16),
            pltpu.VMEM((384, 1280), BF16),
            pltpu.VMEM((10, M1, 128), F32),
            pltpu.VMEM((9, M2, 128), F32),
            pltpu.VMEM((2, 4, M3, 128), F32),
            pltpu.VMEM((2, n, cap, width), BF16),
            pltpu.VMEM((2, n, cap, width), BF16),
            dma((3,)), dma((3,)), dma((n,)), dma((n,)), dma((2, n)), dma((2, n)), dma((8,)), dma(()),
        ],
        compiler_params=pltpu.CompilerParams(
            collective_id=0, has_side_effects=True, vmem_limit_bytes=VMEM1
        ),
    )(
        owner_shift, *arrays, patch_weight,
    )
    placed = pl.pallas_call(
        project,
        name="project",
        out_shape=jax.ShapeDtypeStruct((own, embed), BF16),
        in_specs=[vmem] * 3,
        out_specs=vmem,
        compiler_params=pltpu.CompilerParams(vmem_limit_bytes=16 << 20),
    )(dealt, pw, patch_offset.reshape(-1, 128))
    return placed[None]


def solution(mesh):
    args = (P(None, "strip", "seq"), P("strip", "seq"), P("seq")) + (P(),) * 8
    return jax.shard_map(
        functools.partial(local, mesh.shape["strip"], mesh.shape["seq"]),
        mesh=mesh, in_specs=args, out_specs=P("seq", "strip", None), check_vma=False,
    )
```

```python
import functools

import jax
import jax.numpy as jnp
from jax import lax
from jax.experimental import pallas as pl
from jax.experimental.pallas import tpu as pltpu
from jax.sharding import PartitionSpec as P

MESH = pl.DeviceIdType.MESH
F32 = jnp.float32
BF16 = jnp.bfloat16

M1 = 560
M2 = 272
M3 = 128
VMEM1 = 60000000


def gelu(x):
    return 0.5 * x * (1.0 + lax.erf(x * 0.7071067811865476))


def dot(a, b):
    return jnp.dot(a, b, preferred_element_type=F32)


def dot_nt(a, b):
    return lax.dot_general(a, b, (((1,), (1,)), ((), ())), preferred_element_type=F32)


def kernel(
    n, n_seq, cap,
    shift_ref, img_hbm, flag_hbm, w1_hbm, b1_hbm, w2_hbm, b2_hbm, w3_hbm, b3_hbm, pw_hbm,
    out_ref, pw_out,
    img_ref, flag_ref, w1_ref, b1_ref, w2_ref, b2_ref, w3_ref, b3_ref, top, left, corner, flags, band, slab, slab_t, a1, k1, s1, s2, s3, sendbuf, got,
    halo_send, halo_recv, flag_send, flag_recv, row_send, row_recv, load_sem, pw_sem,
):
    me = lax.axis_index("strip")
    mq = lax.axis_index("seq")
    half = n // 2
    late = me // half
    down, up = lax.rem(me + 1, n), lax.rem(me + n - 1, n)
    right, leftward = lax.rem(mq + 1, n_seq), lax.rem(mq + n_seq - 1, n_seq)

    loads = [
        pltpu.make_async_copy(src, dst, load_sem.at[k])
        for k, (src, dst) in enumerate(
            (
                (w1_hbm, w1_ref), (img_hbm, img_ref), (b1_hbm, b1_ref), (w2_hbm, w2_ref),
                (b2_hbm, b2_ref), (w3_hbm, w3_ref), (b3_hbm, b3_ref), (flag_hbm, flag_ref),
            )
        )
    ]
    barrier = pltpu.get_barrier_semaphore()

    def greet(i, c):
        pl.semaphore_signal(barrier, inc=1, device_id=(lax.rem(me + i, n), mq), device_id_type=MESH)
        return c

    for load in loads[:2]:
        load.start()
    for where in ((me, right), (me, leftward), (down, right), (up, leftward)):
        pl.semaphore_signal(barrier, inc=1, device_id=where, device_id_type=MESH)
    lax.fori_loop(1, n, greet, 0)
    for load in loads[2:]:
        load.start()

    pw_copy = pltpu.make_async_copy(pw_hbm, pw_out, pw_sem)

    def flag_copy(i, source):
        return pltpu.make_async_remote_copy(
            src_ref=flag_hbm, dst_ref=flags.at[source],
            send_sem=flag_send.at[i], recv_sem=flag_recv.at[i],
            device_id=(lax.rem(me + i, n), mq), device_id_type=MESH,
        )

    halos = [
        pltpu.make_async_remote_copy(
            src_ref=src, dst_ref=dst, send_sem=halo_send.at[k], recv_sem=halo_recv.at[k],
            device_id=where, device_id_type=MESH,
        )
        for k, (src, dst, where) in enumerate(
            (
                (img_ref.at[:, 24:32, :], top, (down, mq)),
                (img_ref.at[:, :, 896:1024], left, (me, right)),
                (img_ref.at[:, 24:32, 896:1024], corner, (down, right)),
            )
        )
    ]
    inner_row = me > 0
    inner_col = mq > 0
    to_down, to_right = me < n - 1, mq < n_seq - 1
    sends = (to_down, to_right, jnp.logical_and(to_down, to_right))
    receives = (inner_row, inner_col, jnp.logical_and(inner_row, inner_col))

    def send_flags(i, c):
        flag_copy(i, me).start()
        return c

    def enter():
        pl.semaphore_wait(barrier, n - 1 + 4)
        for halo, sent in zip(halos, sends):
            pl.when(sent)(halo.start)
        lax.fori_loop(1, n, send_flags, 0)

    loads[0].wait()
    low = lax.broadcasted_iota(jnp.int32, (8, 128), 0)
    low_lane = lax.broadcasted_iota(jnp.int32, (8, 128), 1)
    tap = low - 1 - 2 * jnp.where(low_lane >= 64, 1, 0)
    band[...] = jnp.zeros_like(band)
    for dx in range(3):
        tap_w = [w1_ref[3 * dy + dx].astype(F32) for dy in range(3)]
        tap_w = [jnp.concatenate([w, w], axis=1) for w in tap_w]
        for c in range(3):
            block = jnp.zeros((8, 128), F32)
            for dy in range(3):
                block = jnp.where(tap == dy, jnp.broadcast_to(tap_w[dy][c : c + 1], (8, 128)), block)
            band[dx, c, 40:48, :] = block
        for q in range(10):
            parts = [band[dx, c, 40 - 4 * q : 80 - 4 * q, :] for c in range(3)]
            parts = jnp.concatenate(parts + [jnp.zeros((8, 128), F32)], axis=0)
            k1[128 * dx : 128 * dx + 128, 128 * q : 128 * q + 128] = parts.astype(BF16)

    slab[120:128, :] = jnp.zeros((8, 1152), F32)
    slab[:120, 0:128] = jnp.zeros((120, 128), F32)
    loads[1].wait()
    for c in range(3):
        slab[40 * c : 40 * c + 8, 128:1152] = jnp.zeros((8, 1024), F32)
        slab[40 * c + 8 : 40 * c + 40, 128:1152] = img_ref[c].astype(F32)
    slab_t[1152:1280, :] = jnp.zeros((128, 128), F32)

    def fill_a1(tiles, rows):
        for t in tiles:
            slab_t[128 * t : 128 * t + 128, :] = slab[:, 128 * t : 128 * t + 128].T
        for dx in range(3):
            a1[:rows, 128 * dx : 128 * dx + 128] = slab_t[pl.ds(119 + dx, rows, stride=2), :].astype(BF16)

    fill_a1(range(9), M1)
    loads[2].wait()
    b1 = jnp.concatenate([b1_ref[...]] * 4, axis=1)

    def layer_one(t, rows):
        act = gelu(dot(a1[:rows], k1[:, 256 * t : 256 * t + 256]) + b1)
        if t < 2 or rows < M1:
            sub1 = lax.broadcasted_iota(jnp.int32, (rows, 256), 0)
            ok = jnp.logical_or(inner_col, sub1 >= 4)
            if t == 0:
                lane1 = lax.broadcasted_iota(jnp.int32, (rows, 256), 1)
                ok = jnp.logical_and(ok, jnp.logical_or(inner_row, lane1 >= 192))
            act = jnp.where(ok, act, 0.0)
        s1[2 * t, :rows] = act[:, :128]
        s1[2 * t + 1, :rows] = act[:, 128:]

    none = jnp.zeros((64, 128), BF16)

    def tap2(dy, dx):
        return none if dy is None else w2_ref[3 * dy + dx]

    def layer_two(where, rows, pair):
        tiles = (0, 1, 2) if pair else (0, 1)
        order = [(h, dx) for dx in range(3) for h in (0, 1)] + [(2, dx) for dx in range(3) if pair]
        a = jnp.concatenate(
            [
                jnp.concatenate(
                    [s1[r + h, pl.ds(1 + dx, rows, stride=2), :] for r in where], axis=0
                ).astype(BF16)
                for h, dx in order
            ],
            axis=1,
        )
        first = {0: (0, 1), 1: (2, None), 2: (None, None)}
        second = {0: (None, None), 1: (0, 1), 2: (2, None)}
        w2 = []
        for h, dx in order:
            for part in range(2):
                row = [tap2(first[h][part], dx)]
                if pair:
                    row.append(tap2(second[h][part], dx))
                w2.append(jnp.concatenate(row, axis=1))
        summed = dot(a, jnp.concatenate(w2, axis=0))
        bias = jnp.concatenate([b2_ref[...]] * (2 if pair else 1), axis=1)
        act = gelu(summed + bias)
        sub2 = lax.broadcasted_iota(jnp.int32, (rows, 128), 0)
        col_ok2 = jnp.logical_or(inner_col, sub2 >= 1)
        for k, r in enumerate(where):
            for more in range(2 if pair else 1):
                one = act[rows * k : rows * k + rows, 128 * more : 128 * more + 128]
                if r < 4 or rows < M2:
                    ok = jnp.logical_and(col_ok2, inner_row) if r + more == 0 else col_ok2
                    one = jnp.where(ok, one, 0.0)
                s2[r + more, :rows] = one

    def layer_three(where, rows):
        taps = [(dy, dx) for dy in range(3) for dx in range(3)]
        a = jnp.concatenate(
            [
                jnp.concatenate(
                    [s2[2 * r + dy, pl.ds(dx, rows, stride=2), :] for r in where], axis=0
                ).astype(BF16)
                for dy, dx in taps
            ],
            axis=1,
        )
        w3 = jnp.concatenate([w3_ref[3 * dy + dx] for dy, dx in taps], axis=1)
        act = gelu(dot_nt(a, w3) + b3_ref[...])
        for k, r in enumerate(where):
            s3[0, r, :rows] = act[rows * k : rows * k + rows, :128]
            s3[1, r, :rows] = act[rows * k : rows * k + rows, 128:]

    pl.when(late == 1)(enter)
    for t in range(2, 5):
        layer_one(t, M1)
    for load in loads[3:]:
        load.wait()
    pw_copy.start()
    layer_two([4], M2, True)
    layer_two([6], M2, True)
    layer_two([8], M2, False)
    layer_three([2, 3], M3)
    pl.when(late == 0)(enter)

    def receive(k, buf):
        pl.when(receives[k])(halos[k].wait_recv)

        @pl.when(jnp.logical_not(receives[k]))
        def _():
            buf[...] = jnp.zeros_like(buf)

    flags[me] = flag_ref[...]
    own = out_ref.shape[0]
    places = n * cap
    bits = n.bit_length() - 1
    cap_bits = cap.bit_length() - 1
    shift = shift_ref[0]

    def near_flags(i, c):
        source = lax.rem(me + n - i, n)
        flag_copy(i, source).wait()
        return c + flags[source]

    def far_flags(i, c):
        flag_copy(i, lax.rem(me + n - i, n)).wait()
        return c

    def row_copy(pr, i, source):
        return pltpu.make_async_remote_copy(
            src_ref=sendbuf.at[pr, lax.rem(me + i, n)], dst_ref=got.at[pr, source],
            send_sem=row_send.at[pr, i], recv_sem=row_recv.at[pr, i],
            device_id=(lax.rem(me + i, n), mq), device_id_type=MESH,
        )

    def deal(pr, first):
        spot = lax.broadcasted_iota(jnp.int32, (places, 1), 0)
        upper = jnp.where(
            lax.broadcasted_iota(jnp.int32, (64, 64), 0) < lax.broadcasted_iota(jnp.int32, (64, 64), 1),
            1.0, 0.0,
        ).astype(BF16)
        row = flag_ref[pr : pr + 1].astype(F32)
        within = dot(jnp.broadcast_to(row, (16, 64)).astype(BF16), upper)[0:1]
        rank = jnp.where(row > 0.5, within, -1.0).astype(jnp.int32)
        wanted = (((spot >> cap_bits) - shift - first) & (n - 1)) + n * (spot & (cap - 1))
        pick = jnp.where(rank == wanted, 1.0, 0.0).astype(BF16)
        features = jnp.concatenate(
            [
                s3[h, 2 * pr + a, pl.ds(b, 64, stride=2), :].astype(BF16)
                for a in range(2) for b in range(2) for h in range(2)
            ],
            axis=1,
        )
        rows = dot(pick, features)
        sendbuf[pr] = rows.reshape(n, cap, rows.shape[1]).astype(BF16)

        def send_rows(i, c):
            row_copy(pr, i, me).start()
            return c

        lax.fori_loop(1, n, send_rows, 0)
        got[pr, me] = sendbuf[pr, me]

    receive(1, left)
    for c in range(3):
        slab[40 * c + 8 : 40 * c + 40, 0:128] = left[c].astype(F32)
    fill_a1(range(1), 16)
    for t in range(2, 5):
        layer_one(t, 16)
    layer_two([4, 6], 8, True)
    layer_two([8], 8, False)
    layer_three([2, 3], 8)
    near = lax.fori_loop(
        1 + late * me, me + 1 + late * (n - me - 1), near_flags, jnp.zeros(flag_ref.shape, jnp.int32)
    )
    near = jnp.sum(near.astype(F32))
    mine = [jnp.sum(flag_ref[pr : pr + 1].astype(F32), axis=1, keepdims=True) for pr in range(2)]
    start = jnp.where(late == 1, n * own - near - mine[0] - mine[1], near + jnp.zeros((1, 1), F32))
    deal(1, (start + mine[0]).astype(jnp.int32))

    receive(0, top)
    receive(2, corner)
    for c in range(3):
        slab[40 * c : 40 * c + 8, 128:1152] = top[c].astype(F32)
        slab[40 * c : 40 * c + 8, 0:128] = corner[c].astype(F32)
    fill_a1(range(9), M1)
    for t in range(2):
        layer_one(t, M1)
    layer_two([0], M2, True)
    layer_two([2], M2, True)
    layer_three([0, 1], M3)
    deal(0, start.astype(jnp.int32))

    lax.fori_loop(me + 1 - late * me, n - late * (n - me - 1), far_flags, 0)
    src_of = lax.broadcasted_iota(jnp.int32, (n, places), 1) >> cap_bits
    src_at = lax.broadcasted_iota(jnp.int32, (n, places), 0)
    same = jnp.where(src_at == src_of, 1.0, 0.0).astype(BF16)
    earlier = jnp.where(src_at < src_of, 1.0, 0.0).astype(BF16)
    turn = lax.broadcasted_iota(jnp.int32, (1, places), 1) & (cap - 1)
    slots = lax.broadcasted_iota(jnp.int32, (own, places), 0)
    counts = [
        dot_nt(jnp.ones((8, 64), BF16), flags[:, pr, :].astype(F32).astype(BF16)).astype(BF16)
        for pr in range(2)
    ]
    count_l = [dot(part, same)[0:1].astype(jnp.int32) for part in counts]
    start_l = dot(counts[0], earlier)[0:1] + dot(counts[1], earlier)[0:1]
    start_l = start_l.astype(jnp.int32)
    place = []
    for pr in range(2):
        rank_l = ((me - shift - start_l) & (n - 1)) + n * turn
        slot_l = jnp.where(rank_l < count_l[pr], (start_l + rank_l) >> bits, -1)
        place.append(jnp.where(slots == slot_l, 1.0, 0.0).astype(BF16))
        start_l = start_l + count_l[pr]
    filled = jnp.sum(place[0].astype(F32), axis=1, keepdims=True)
    filled = filled + jnp.sum(place[1].astype(F32), axis=1, keepdims=True)
    width = got.shape[3]
    out_ref[:, width:] = jnp.broadcast_to(filled, (own, 128)).astype(BF16)

    placed = None
    for pr in (1, 0):

        def wait_rows(i, c, pr=pr):
            row_copy(pr, i, lax.rem(me + n - i, n)).wait()
            return c

        lax.fori_loop(1, n, wait_rows, 0)
        rows = got[pr].astype(F32).reshape(places, width).astype(BF16)
        part = dot(place[pr], rows)
        placed = part if placed is None else placed + part
    out_ref[:, :width] = placed.astype(BF16)
    for halo, sent in zip(halos, sends):
        pl.when(sent)(halo.wait_send)
    pw_copy.wait()


def project(dealt_ref, pw_ref, pb_ref, out_ref):
    width = pw_ref.shape[0] * pw_ref.shape[1]
    filled = dealt_ref[:, width:].astype(F32)
    filled = jnp.concatenate([filled, filled], axis=1)
    for t in range(6):
        cut = slice(256 * t, 256 * t + 256)
        summed = None
        for k in range(4):
            part = dot(dealt_ref[:, 256 * k : 256 * k + 256], pw_ref[k, :, cut])
            summed = part if summed is None else summed + part
        bias = jnp.concatenate([pb_ref[2 * t : 2 * t + 1], pb_ref[2 * t + 1 : 2 * t + 2]], axis=1)
        out_ref[:, cut] = jnp.where(filled > 0.5, summed + bias, 0.0).astype(BF16)


def local(n, n_seq, slide_image, keep_flags, owner_shift, weight_one, offset_one, weight_two,
          offset_two, weight_three, offset_three, patch_weight, patch_offset):
    patches = keep_flags.size
    embed = patch_weight.shape[2]
    cap = 8 * -(-(-(-keep_flags.shape[1] // n)) // 8)
    width = patch_weight.shape[0] * patch_weight.shape[1]
    arrays = (
        slide_image, keep_flags, weight_one.transpose(0, 2, 1), offset_one[None],
        weight_two.transpose(0, 2, 1), offset_two[None], weight_three, offset_three[None],
    )
    own = patches // 2
    vmem = pl.BlockSpec(memory_space=pltpu.VMEM)
    anywhere = pl.BlockSpec(memory_space=pltpu.HBM)
    dma = pltpu.SemaphoreType.DMA
    dealt, pw = pl.pallas_call(
        functools.partial(kernel, n, n_seq, cap),
        name="stem_and_deal",
        out_shape=(
            pltpu.VMEM((own, width + 128), BF16),
            pltpu.VMEM(patch_weight.shape, BF16),
        ),
        in_specs=[pl.BlockSpec(memory_space=pltpu.SMEM)] + [anywhere] * 9,
        out_specs=(vmem, pl.BlockSpec(memory_space=pltpu.VMEM)),
        scratch_shapes=[
            *(pltpu.VMEM(x.shape, x.dtype) for x in arrays),
            pltpu.VMEM((3, 8, 1024), BF16),
            pltpu.VMEM((3, 32, 128), BF16),
            pltpu.VMEM((3, 8, 128), BF16),
            pltpu.VMEM((n,) + keep_flags.shape, jnp.int32),
            pltpu.VMEM((3, 3, 80, 128), F32),
            pltpu.VMEM((128, 1152), F32),
            pltpu.VMEM((1280, 128), F32),
            pltpu.VMEM((M1, 384), BF16),
            pltpu.VMEM((384, 1280), BF16),
            pltpu.VMEM((10, M1, 128), F32),
            pltpu.VMEM((9, M2, 128), F32),
            pltpu.VMEM((2, 4, M3, 128), F32),
            pltpu.VMEM((2, n, cap, width), BF16),
            pltpu.VMEM((2, n, cap, width), BF16),
            dma((3,)), dma((3,)), dma((n,)), dma((n,)), dma((2, n)), dma((2, n)), dma((8,)), dma(()),
        ],
        compiler_params=pltpu.CompilerParams(
            collective_id=0, has_side_effects=True, vmem_limit_bytes=VMEM1
        ),
    )(
        owner_shift, *arrays, patch_weight,
    )
    placed = pl.pallas_call(
        project,
        name="project",
        out_shape=jax.ShapeDtypeStruct((own, embed), BF16),
        in_specs=[vmem] * 3,
        out_specs=vmem,
        compiler_params=pltpu.CompilerParams(vmem_limit_bytes=16 << 20),
    )(dealt, pw, patch_offset.reshape(-1, 128))
    return placed[None]


def solution(mesh):
    args = (P(None, "strip", "seq"), P("strip", "seq"), P("seq")) + (P(),) * 8
    return jax.shard_map(
        functools.partial(local, mesh.shape["strip"], mesh.shape["seq"]),
        mesh=mesh, in_specs=args, out_specs=P("seq", "strip", None), check_vma=False,
    )
```

```python
import functools

import jax
import jax.numpy as jnp
from jax import lax
from jax.experimental import pallas as pl
from jax.experimental.pallas import tpu as pltpu
from jax.sharding import PartitionSpec as P

MESH = pl.DeviceIdType.MESH
F32 = jnp.float32
BF16 = jnp.bfloat16

M1 = 528
M2 = 272
M3 = 128
VMEM1 = 60000000


def gelu(x):
    return 0.5 * x * (1.0 + lax.erf(x * 0.7071067811865476))


def dot(a, b):
    return jnp.dot(a, b, preferred_element_type=F32)


def dot_nt(a, b):
    return lax.dot_general(a, b, (((1,), (1,)), ((), ())), preferred_element_type=F32)


def kernel(
    n, n_seq, cap,
    shift_ref, img_hbm, flag_hbm, w1_hbm, b1_hbm, w2_hbm, b2_hbm, w3_hbm, b3_hbm, pw_hbm,
    out_ref, pw_out,
    img_ref, flag_ref, w1_ref, b1_ref, w2_ref, b2_ref, w3_ref, b3_ref, top, left, corner, flags, band, slab, slab_t, a1, k1, s1, s2, s3, sendbuf, got,
    halo_send, halo_recv, flag_send, flag_recv, row_send, row_recv, load_sem, pw_sem,
):
    me = lax.axis_index("strip")
    mq = lax.axis_index("seq")
    half = n // 2
    late = me // half
    down, up = lax.rem(me + 1, n), lax.rem(me + n - 1, n)
    right, leftward = lax.rem(mq + 1, n_seq), lax.rem(mq + n_seq - 1, n_seq)

    loads = [
        pltpu.make_async_copy(src, dst, load_sem.at[k])
        for k, (src, dst) in enumerate(
            (
                (w1_hbm, w1_ref), (img_hbm, img_ref), (b1_hbm, b1_ref), (w2_hbm, w2_ref),
                (b2_hbm, b2_ref), (w3_hbm, w3_ref), (b3_hbm, b3_ref), (flag_hbm, flag_ref),
            )
        )
    ]
    barrier = pltpu.get_barrier_semaphore()

    def greet(i, c):
        pl.semaphore_signal(barrier, inc=1, device_id=(lax.rem(me + i, n), mq), device_id_type=MESH)
        return c

    for load in loads[:2]:
        load.start()
    for where in ((me, right), (me, leftward), (down, right), (up, leftward)):
        pl.semaphore_signal(barrier, inc=1, device_id=where, device_id_type=MESH)
    lax.fori_loop(1, n, greet, 0)
    for load in loads[2:]:
        load.start()

    pw_copy = pltpu.make_async_copy(pw_hbm, pw_out, pw_sem)

    def flag_copy(i, source):
        return pltpu.make_async_remote_copy(
            src_ref=flag_hbm, dst_ref=flags.at[source],
            send_sem=flag_send.at[i], recv_sem=flag_recv.at[i],
            device_id=(lax.rem(me + i, n), mq), device_id_type=MESH,
        )

    halos = [
        pltpu.make_async_remote_copy(
            src_ref=src, dst_ref=dst, send_sem=halo_send.at[k], recv_sem=halo_recv.at[k],
            device_id=where, device_id_type=MESH,
        )
        for k, (src, dst, where) in enumerate(
            (
                (img_ref.at[:, 24:32, :], top, (down, mq)),
                (img_ref.at[:, :, 896:1024], left, (me, right)),
                (img_ref.at[:, 24:32, 896:1024], corner, (down, right)),
            )
        )
    ]
    inner_row = me > 0
    inner_col = mq > 0
    to_down, to_right = me < n - 1, mq < n_seq - 1
    sends = (to_down, to_right, jnp.logical_and(to_down, to_right))
    receives = (inner_row, inner_col, jnp.logical_and(inner_row, inner_col))

    def send_flags(i, c):
        flag_copy(i, me).start()
        return c

    def enter():
        pl.semaphore_wait(barrier, n - 1 + 4)
        for halo, sent in zip(halos, sends):
            pl.when(sent)(halo.start)
        lax.fori_loop(1, n, send_flags, 0)

    loads[0].wait()
    low = lax.broadcasted_iota(jnp.int32, (8, 128), 0)
    low_lane = lax.broadcasted_iota(jnp.int32, (8, 128), 1)
    tap = low - 1 - 2 * jnp.where(low_lane >= 64, 1, 0)
    band[...] = jnp.zeros_like(band)
    for dx in range(3):
        tap_w = [w1_ref[3 * dy + dx].astype(F32) for dy in range(3)]
        tap_w = [jnp.concatenate([w, w], axis=1) for w in tap_w]
        for c in range(3):
            block = jnp.zeros((8, 128), F32)
            for dy in range(3):
                block = jnp.where(tap == dy, jnp.broadcast_to(tap_w[dy][c : c + 1], (8, 128)), block)
            band[dx, c, 40:48, :] = block
    for q in range(6):
        parts = [band[dx, c, 40 - 4 * q : 64 - 4 * q, :] for dx in range(3) for c in range(3)]
        parts = jnp.concatenate(parts + [jnp.zeros((40, 128), F32)], axis=0)
        k1[:, 128 * q : 128 * q + 128] = parts.astype(BF16)

    slab[216:256, :] = jnp.zeros((40, 1280), F32)
    slab[:72, 0:128] = jnp.zeros((72, 128), F32)
    slab[:72, 1152:1280] = jnp.zeros((72, 128), F32)
    slab_t[:, 1152:1280, :] = jnp.zeros((2, 128, 128), F32)
    loads[1].wait()
    for c in range(3):
        slab[24 * c : 24 * c + 24, 128:1152] = img_ref[c, 8:32].astype(F32)

    def fill_a1(tiles, rows):
        wide = min(1280, 128 * tiles + 128)
        base = slab[:72, :wide]
        for dx in range(1, 3):
            moved = pltpu.roll(base, wide - dx, axis=1)
            slab[72 * dx : 72 * dx + 72, : 128 * tiles] = moved[:, : 128 * tiles]
        for t in range(tiles):
            for k in range(2):
                slab_t[k, 128 * t : 128 * t + 128, :] = slab[
                    128 * k : 128 * k + 128, 128 * t : 128 * t + 128
                ].T
        for k in range(2):
            a1[:rows, 128 * k : 128 * k + 128] = slab_t[k, pl.ds(119, rows, stride=2), :].astype(BF16)

    fill_a1(9, M1)
    loads[2].wait()
    b1 = jnp.concatenate([b1_ref[...]] * 4, axis=1)

    def layer_one(t, rows):
        act = gelu(dot(a1[:rows], k1[:, 256 * (t % 2 + t // 4 * 2) : 256 * (t % 2 + t // 4 * 2) + 256]) + b1)
        if t < 2 or rows < M1:
            sub1 = lax.broadcasted_iota(jnp.int32, (rows, 256), 0)
            ok = jnp.logical_or(inner_col, sub1 >= 4)
            if t == 0:
                lane1 = lax.broadcasted_iota(jnp.int32, (rows, 256), 1)
                ok = jnp.logical_and(ok, jnp.logical_or(inner_row, lane1 >= 192))
            act = jnp.where(ok, act, 0.0)
        s1[2 * t, :rows] = act[:, :128]
        s1[2 * t + 1, :rows] = act[:, 128:]

    none = jnp.zeros((64, 128), BF16)

    def tap2(dy, dx):
        return none if dy is None else w2_ref[3 * dy + dx]

    def layer_two(where, rows, pair):
        tiles = (0, 1, 2) if pair else (0, 1)
        order = [(h, dx) for dx in range(3) for h in (0, 1)] + [(2, dx) for dx in range(3) if pair]
        a = jnp.concatenate(
            [
                jnp.concatenate(
                    [s1[r + h, pl.ds(1 + dx, rows, stride=2), :] for r in where], axis=0
                ).astype(BF16)
                for h, dx in order
            ],
            axis=1,
        )
        first = {0: (0, 1), 1: (2, None), 2: (None, None)}
        second = {0: (None, None), 1: (0, 1), 2: (2, None)}
        w2 = []
        for h, dx in order:
            for part in range(2):
                row = [tap2(first[h][part], dx)]
                if pair:
                    row.append(tap2(second[h][part], dx))
                w2.append(jnp.concatenate(row, axis=1))
        summed = dot(a, jnp.concatenate(w2, axis=0))
        bias = jnp.concatenate([b2_ref[...]] * (2 if pair else 1), axis=1)
        act = gelu(summed + bias)
        sub2 = lax.broadcasted_iota(jnp.int32, (rows, 128), 0)
        col_ok2 = jnp.logical_or(inner_col, sub2 >= 1)
        for k, r in enumerate(where):
            for more in range(2 if pair else 1):
                one = act[rows * k : rows * k + rows, 128 * more : 128 * more + 128]
                if r < 4 or rows < M2:
                    ok = jnp.logical_and(col_ok2, inner_row) if r + more == 0 else col_ok2
                    one = jnp.where(ok, one, 0.0)
                s2[r + more, :rows] = one

    def layer_three(where, rows):
        taps = [(dy, dx) for dy in range(3) for dx in range(3)]
        a = jnp.concatenate(
            [
                jnp.concatenate(
                    [s2[2 * r + dy, pl.ds(dx, rows, stride=2), :] for r in where], axis=0
                ).astype(BF16)
                for dy, dx in taps
            ],
            axis=1,
        )
        w3 = jnp.concatenate([w3_ref[3 * dy + dx] for dy, dx in taps], axis=1)
        act = gelu(dot_nt(a, w3) + b3_ref[...])
        for k, r in enumerate(where):
            s3[0, r, :rows] = act[rows * k : rows * k + rows, :128]
            s3[1, r, :rows] = act[rows * k : rows * k + rows, 128:]

    pl.when(late == 1)(enter)
    for t in range(2, 5):
        layer_one(t, M1)
    for load in loads[3:]:
        load.wait()
    pw_copy.start()
    layer_two([4], M2, True)
    layer_two([6], M2, True)
    layer_two([8], M2, False)
    layer_three([2, 3], M3)
    pl.when(late == 0)(enter)

    def receive(k, buf):
        pl.when(receives[k])(halos[k].wait_recv)

        @pl.when(jnp.logical_not(receives[k]))
        def _():
            buf[...] = jnp.zeros_like(buf)

    flags[me] = flag_ref[...]
    own = out_ref.shape[0]
    places = n * cap
    bits = n.bit_length() - 1
    cap_bits = cap.bit_length() - 1
    shift = shift_ref[0]

    def near_flags(i, c):
        source = lax.rem(me + n - i, n)
        flag_copy(i, source).wait()
        return c + flags[source]

    def far_flags(i, c):
        flag_copy(i, lax.rem(me + n - i, n)).wait()
        return c

    def row_copy(pr, i, source):
        return pltpu.make_async_remote_copy(
            src_ref=sendbuf.at[pr, lax.rem(me + i, n)], dst_ref=got.at[pr, source],
            send_sem=row_send.at[pr, i], recv_sem=row_recv.at[pr, i],
            device_id=(lax.rem(me + i, n), mq), device_id_type=MESH,
        )

    def deal(pr, first):
        spot = lax.broadcasted_iota(jnp.int32, (places, 1), 0)
        upper = jnp.where(
            lax.broadcasted_iota(jnp.int32, (64, 64), 0) < lax.broadcasted_iota(jnp.int32, (64, 64), 1),
            1.0, 0.0,
        ).astype(BF16)
        row = flag_ref[pr : pr + 1].astype(F32)
        within = dot(jnp.broadcast_to(row, (16, 64)).astype(BF16), upper)[0:1]
        rank = jnp.where(row > 0.5, within, -1.0).astype(jnp.int32)
        wanted = (((spot >> cap_bits) - shift - first) & (n - 1)) + n * (spot & (cap - 1))
        pick = jnp.where(rank == wanted, 1.0, 0.0).astype(BF16)
        features = jnp.concatenate(
            [
                s3[h, 2 * pr + a, pl.ds(b, 64, stride=2), :].astype(BF16)
                for a in range(2) for b in range(2) for h in range(2)
            ],
            axis=1,
        )
        rows = dot(pick, features)
        sendbuf[pr] = rows.reshape(n, cap, rows.shape[1]).astype(BF16)

        def send_rows(i, c):
            row_copy(pr, i, me).start()
            return c

        lax.fori_loop(1, n, send_rows, 0)
        got[pr, me] = sendbuf[pr, me]

    receive(1, left)
    for c in range(3):
        slab[24 * c : 24 * c + 24, 0:128] = left[c, 8:32].astype(F32)
    fill_a1(1, 16)
    for t in range(2, 5):
        layer_one(t, 16)
    layer_two([4, 6], 8, True)
    layer_two([8], 8, False)
    layer_three([2, 3], 8)
    near = lax.fori_loop(
        1 + late * me, me + 1 + late * (n - me - 1), near_flags, jnp.zeros(flag_ref.shape, jnp.int32)
    )
    near = jnp.sum(near.astype(F32))
    mine = [jnp.sum(flag_ref[pr : pr + 1].astype(F32), axis=1, keepdims=True) for pr in range(2)]
    start = jnp.where(late == 1, n * own - near - mine[0] - mine[1], near + jnp.zeros((1, 1), F32))
    deal(1, (start + mine[0]).astype(jnp.int32))

    receive(0, top)
    receive(2, corner)
    for c in range(3):
        slab[24 * c : 24 * c + 8, 128:1152] = top[c].astype(F32)
        slab[24 * c : 24 * c + 8, 0:128] = corner[c].astype(F32)
        slab[24 * c + 8 : 24 * c + 24, 128:1152] = img_ref[c, 0:16].astype(F32)
        slab[24 * c + 8 : 24 * c + 24, 0:128] = left[c, 0:16].astype(F32)
    fill_a1(9, M1)
    for t in range(2):
        layer_one(t, M1)
    layer_two([0], M2, True)
    layer_two([2], M2, True)
    layer_three([0, 1], M3)
    deal(0, start.astype(jnp.int32))

    lax.fori_loop(me + 1 - late * me, n - late * (n - me - 1), far_flags, 0)
    src_of = lax.broadcasted_iota(jnp.int32, (n, places), 1) >> cap_bits
    src_at = lax.broadcasted_iota(jnp.int32, (n, places), 0)
    same = jnp.where(src_at == src_of, 1.0, 0.0).astype(BF16)
    earlier = jnp.where(src_at < src_of, 1.0, 0.0).astype(BF16)
    turn = lax.broadcasted_iota(jnp.int32, (1, places), 1) & (cap - 1)
    slots = lax.broadcasted_iota(jnp.int32, (own, places), 0)
    counts = [
        dot_nt(jnp.ones((8, 64), BF16), flags[:, pr, :].astype(F32).astype(BF16)).astype(BF16)
        for pr in range(2)
    ]
    count_l = [dot(part, same)[0:1].astype(jnp.int32) for part in counts]
    start_l = dot(counts[0], earlier)[0:1] + dot(counts[1], earlier)[0:1]
    start_l = start_l.astype(jnp.int32)
    place = []
    for pr in range(2):
        rank_l = ((me - shift - start_l) & (n - 1)) + n * turn
        slot_l = jnp.where(rank_l < count_l[pr], (start_l + rank_l) >> bits, -1)
        place.append(jnp.where(slots == slot_l, 1.0, 0.0).astype(BF16))
        start_l = start_l + count_l[pr]
    filled = jnp.sum(place[0].astype(F32), axis=1, keepdims=True)
    filled = filled + jnp.sum(place[1].astype(F32), axis=1, keepdims=True)
    width = got.shape[3]
    out_ref[:, width:] = jnp.broadcast_to(filled, (own, 128)).astype(BF16)

    placed = None
    for pr in (1, 0):

        def wait_rows(i, c, pr=pr):
            row_copy(pr, i, lax.rem(me + n - i, n)).wait()
            return c

        lax.fori_loop(1, n, wait_rows, 0)
        rows = got[pr].astype(F32).reshape(places, width).astype(BF16)
        part = dot(place[pr], rows)
        placed = part if placed is None else placed + part
    out_ref[:, :width] = placed.astype(BF16)
    for halo, sent in zip(halos, sends):
        pl.when(sent)(halo.wait_send)
    pw_copy.wait()


def project(dealt_ref, pw_ref, pb_ref, out_ref):
    width = pw_ref.shape[0] * pw_ref.shape[1]
    filled = dealt_ref[:, width:].astype(F32)
    filled = jnp.concatenate([filled, filled], axis=1)
    for t in range(6):
        cut = slice(256 * t, 256 * t + 256)
        summed = None
        for k in range(4):
            part = dot(dealt_ref[:, 256 * k : 256 * k + 256], pw_ref[k, :, cut])
            summed = part if summed is None else summed + part
        bias = jnp.concatenate([pb_ref[2 * t : 2 * t + 1], pb_ref[2 * t + 1 : 2 * t + 2]], axis=1)
        out_ref[:, cut] = jnp.where(filled > 0.5, summed + bias, 0.0).astype(BF16)


def local(n, n_seq, slide_image, keep_flags, owner_shift, weight_one, offset_one, weight_two,
          offset_two, weight_three, offset_three, patch_weight, patch_offset):
    patches = keep_flags.size
    embed = patch_weight.shape[2]
    cap = 8 * -(-(-(-keep_flags.shape[1] // n)) // 8)
    width = patch_weight.shape[0] * patch_weight.shape[1]
    arrays = (
        slide_image, keep_flags, weight_one.transpose(0, 2, 1), offset_one[None],
        weight_two.transpose(0, 2, 1), offset_two[None], weight_three, offset_three[None],
    )
    own = patches // 2
    vmem = pl.BlockSpec(memory_space=pltpu.VMEM)
    anywhere = pl.BlockSpec(memory_space=pltpu.HBM)
    dma = pltpu.SemaphoreType.DMA
    dealt, pw = pl.pallas_call(
        functools.partial(kernel, n, n_seq, cap),
        name="stem_and_deal",
        out_shape=(
            pltpu.VMEM((own, width + 128), BF16),
            pltpu.VMEM(patch_weight.shape, BF16),
        ),
        in_specs=[pl.BlockSpec(memory_space=pltpu.SMEM)] + [anywhere] * 9,
        out_specs=(vmem, pl.BlockSpec(memory_space=pltpu.VMEM)),
        scratch_shapes=[
            *(pltpu.VMEM(x.shape, x.dtype) for x in arrays),
            pltpu.VMEM((3, 8, 1024), BF16),
            pltpu.VMEM((3, 32, 128), BF16),
            pltpu.VMEM((3, 8, 128), BF16),
            pltpu.VMEM((n,) + keep_flags.shape, jnp.int32),
            pltpu.VMEM((3, 3, 80, 128), F32),
            pltpu.VMEM((256, 1280), F32),
            pltpu.VMEM((2, 1280, 128), F32),
            pltpu.VMEM((M1, 256), BF16),
            pltpu.VMEM((256, 768), BF16),
            pltpu.VMEM((10, 560, 128), F32),
            pltpu.VMEM((9, M2, 128), F32),
            pltpu.VMEM((2, 4, M3, 128), F32),
            pltpu.VMEM((2, n, cap, width), BF16),
            pltpu.VMEM((2, n, cap, width), BF16),
            dma((3,)), dma((3,)), dma((n,)), dma((n,)), dma((2, n)), dma((2, n)), dma((8,)), dma(()),
        ],
        compiler_params=pltpu.CompilerParams(
            collective_id=0, has_side_effects=True, vmem_limit_bytes=VMEM1
        ),
    )(
        owner_shift, *arrays, patch_weight,
    )
    placed = pl.pallas_call(
        project,
        name="project",
        out_shape=jax.ShapeDtypeStruct((own, embed), BF16),
        in_specs=[vmem] * 3,
        out_specs=vmem,
        compiler_params=pltpu.CompilerParams(vmem_limit_bytes=16 << 20),
    )(dealt, pw, patch_offset.reshape(-1, 128))
    return placed[None]


def solution(mesh):
    args = (P(None, "strip", "seq"), P("strip", "seq"), P("seq")) + (P(),) * 8
    return jax.shard_map(
        functools.partial(local, mesh.shape["strip"], mesh.shape["seq"]),
        mesh=mesh, in_specs=args, out_specs=P("seq", "strip", None), check_vma=False,
    )
```

```python
import functools

import jax
import jax.numpy as jnp
from jax import lax
from jax.experimental import pallas as pl
from jax.experimental.pallas import tpu as pltpu
from jax.sharding import PartitionSpec as P

MESH = pl.DeviceIdType.MESH
F32 = jnp.float32
BF16 = jnp.bfloat16

M1 = 528
M2 = 272
M3 = 128
VMEM1 = 60000000


def gelu(x):
    return 0.5 * x * (1.0 + lax.erf(x * 0.7071067811865476))


def dot(a, b):
    return jnp.dot(a, b, preferred_element_type=F32)


def dot_nt(a, b):
    return lax.dot_general(a, b, (((1,), (1,)), ((), ())), preferred_element_type=F32)


def kernel(
    n, n_seq, cap,
    shift_ref, img_hbm, flag_hbm, w1_hbm, b1_hbm, w2_hbm, b2_hbm, w3_hbm, b3_hbm, pw_hbm,
    out_ref, pw_out,
    img_ref, flag_ref, w1_ref, b1_ref, w2_ref, b2_ref, w3_ref, b3_ref, top, left, corner, flags, band, slab, slab_t, a1, k1, s1, s2, s3, sendbuf, got,
    halo_send, halo_recv, flag_send, flag_recv, row_send, row_recv, load_sem, pw_sem,
):
    me = lax.axis_index("strip")
    mq = lax.axis_index("seq")
    half = n // 2
    late = me // half
    down, up = lax.rem(me + 1, n), lax.rem(me + n - 1, n)
    right, leftward = lax.rem(mq + 1, n_seq), lax.rem(mq + n_seq - 1, n_seq)

    loads = [
        pltpu.make_async_copy(src, dst, load_sem.at[k])
        for k, (src, dst) in enumerate(
            (
                (w1_hbm, w1_ref), (img_hbm, img_ref), (b1_hbm, b1_ref), (w2_hbm, w2_ref),
                (b2_hbm, b2_ref), (w3_hbm, w3_ref), (b3_hbm, b3_ref), (flag_hbm, flag_ref),
            )
        )
    ]
    barrier = pltpu.get_barrier_semaphore()

    def greet(i, c):
        pl.semaphore_signal(barrier, inc=1, device_id=(lax.rem(me + i, n), mq), device_id_type=MESH)
        return c

    for load in loads[:2]:
        load.start()
    for where in ((me, right), (me, leftward), (down, right), (up, leftward)):
        pl.semaphore_signal(barrier, inc=1, device_id=where, device_id_type=MESH)
    lax.fori_loop(1, n, greet, 0)
    for load in loads[2:]:
        load.start()

    pw_copy = pltpu.make_async_copy(pw_hbm, pw_out, pw_sem)

    def flag_copy(i, source):
        return pltpu.make_async_remote_copy(
            src_ref=flag_hbm, dst_ref=flags.at[source],
            send_sem=flag_send.at[i], recv_sem=flag_recv.at[i],
            device_id=(lax.rem(me + i, n), mq), device_id_type=MESH,
        )

    halos = [
        pltpu.make_async_remote_copy(
            src_ref=src, dst_ref=dst, send_sem=halo_send.at[k], recv_sem=halo_recv.at[k],
            device_id=where, device_id_type=MESH,
        )
        for k, (src, dst, where) in enumerate(
            (
                (img_ref.at[:, 24:32, :], top, (down, mq)),
                (img_ref.at[:, :, 896:1024], left, (me, right)),
                (img_ref.at[:, 24:32, 896:1024], corner, (down, right)),
            )
        )
    ]
    inner_row = me > 0
    inner_col = mq > 0
    to_down, to_right = me < n - 1, mq < n_seq - 1
    sends = (to_down, to_right, jnp.logical_and(to_down, to_right))
    receives = (inner_row, inner_col, jnp.logical_and(inner_row, inner_col))

    def send_flags(i, c):
        flag_copy(i, me).start()
        return c

    def enter():
        pl.semaphore_wait(barrier, n - 1 + 4)
        for halo, sent in zip(halos, sends):
            pl.when(sent)(halo.start)
        lax.fori_loop(1, n, send_flags, 0)

    loads[0].wait()
    low = lax.broadcasted_iota(jnp.int32, (8, 128), 0)
    low_lane = lax.broadcasted_iota(jnp.int32, (8, 128), 1)
    tap = low - 1 - 2 * jnp.where(low_lane >= 64, 1, 0)
    band[...] = jnp.zeros_like(band)
    for dx in range(3):
        tap_w = [w1_ref[3 * dy + dx].astype(F32) for dy in range(3)]
        tap_w = [jnp.concatenate([w, w], axis=1) for w in tap_w]
        for c in range(3):
            block = jnp.zeros((8, 128), F32)
            for dy in range(3):
                block = jnp.where(tap == dy, jnp.broadcast_to(tap_w[dy][c : c + 1], (8, 128)), block)
            band[dx, c, 40:48, :] = block
    for q in range(6):
        parts = [band[dx, c, 40 - 4 * q : 64 - 4 * q, :] for dx in range(3) for c in range(3)]
        parts = jnp.concatenate(parts + [jnp.zeros((40, 128), F32)], axis=0)
        k1[:, 128 * q : 128 * q + 128] = parts.astype(BF16)

    slab[:, 0:128] = jnp.zeros((72, 128), F32)
    slab_t[...] = jnp.zeros_like(slab_t)
    loads[1].wait()
    for c in range(3):
        slab[24 * c : 24 * c + 24, 128:1152] = img_ref[c, 8:32].astype(F32)

    def fill_a1(tiles, rows):
        for t in range(tiles):
            slab_t[128 * t : 128 * t + 128, 0:72] = slab[:, 128 * t : 128 * t + 128].T
        one, two, three = [slab_t[pl.ds(119 + dx, rows, stride=2), :] for dx in range(3)]
        two = pltpu.roll(two, 72, axis=1)
        three = pltpu.roll(three, 16, axis=1)
        lane = lax.broadcasted_iota(jnp.int32, (rows, 128), 1)
        a1[:rows, 0:128] = jnp.where(lane < 72, one, two).astype(BF16)
        a1[:rows, 128:256] = jnp.where(lane < 16, two, three).astype(BF16)

    fill_a1(9, M1)
    loads[2].wait()
    b1 = jnp.concatenate([b1_ref[...]] * 4, axis=1)

    def layer_one(t, rows):
        act = gelu(dot(a1[:rows], k1[:, 256 * (t % 2 + t // 4 * 2) : 256 * (t % 2 + t // 4 * 2) + 256]) + b1)
        if t < 2 or rows < M1:
            sub1 = lax.broadcasted_iota(jnp.int32, (rows, 256), 0)
            ok = jnp.logical_or(inner_col, sub1 >= 4)
            if t == 0:
                lane1 = lax.broadcasted_iota(jnp.int32, (rows, 256), 1)
                ok = jnp.logical_and(ok, jnp.logical_or(inner_row, lane1 >= 192))
            act = jnp.where(ok, act, 0.0)
        s1[2 * t, :rows] = act[:, :128]
        s1[2 * t + 1, :rows] = act[:, 128:]

    none = jnp.zeros((64, 128), BF16)

    def tap2(dy, dx):
        return none if dy is None else w2_ref[3 * dy + dx]

    def layer_two(where, rows, pair):
        tiles = (0, 1, 2) if pair else (0, 1)
        order = [(h, dx) for dx in range(3) for h in (0, 1)] + [(2, dx) for dx in range(3) if pair]
        a = jnp.concatenate(
            [
                jnp.concatenate(
                    [s1[r + h, pl.ds(1 + dx, rows, stride=2), :] for r in where], axis=0
                ).astype(BF16)
                for h, dx in order
            ],
            axis=1,
        )
        first = {0: (0, 1), 1: (2, None), 2: (None, None)}
        second = {0: (None, None), 1: (0, 1), 2: (2, None)}
        w2 = []
        for h, dx in order:
            for part in range(2):
                row = [tap2(first[h][part], dx)]
                if pair:
                    row.append(tap2(second[h][part], dx))
                w2.append(jnp.concatenate(row, axis=1))
        summed = dot(a, jnp.concatenate(w2, axis=0))
        bias = jnp.concatenate([b2_ref[...]] * (2 if pair else 1), axis=1)
        act = gelu(summed + bias)
        sub2 = lax.broadcasted_iota(jnp.int32, (rows, 128), 0)
        col_ok2 = jnp.logical_or(inner_col, sub2 >= 1)
        for k, r in enumerate(where):
            for more in range(2 if pair else 1):
                one = act[rows * k : rows * k + rows, 128 * more : 128 * more + 128]
                if r < 4 or rows < M2:
                    ok = jnp.logical_and(col_ok2, inner_row) if r + more == 0 else col_ok2
                    one = jnp.where(ok, one, 0.0)
                s2[r + more, :rows] = one

    def layer_three(where, rows):
        taps = [(dy, dx) for dy in range(3) for dx in range(3)]
        a = jnp.concatenate(
            [
                jnp.concatenate(
                    [s2[2 * r + dy, pl.ds(dx, rows, stride=2), :] for r in where], axis=0
                ).astype(BF16)
                for dy, dx in taps
            ],
            axis=1,
        )
        w3 = jnp.concatenate([w3_ref[3 * dy + dx] for dy, dx in taps], axis=1)
        act = gelu(dot_nt(a, w3) + b3_ref[...])
        for k, r in enumerate(where):
            s3[0, r, :rows] = act[rows * k : rows * k + rows, :128]
            s3[1, r, :rows] = act[rows * k : rows * k + rows, 128:]

    pl.when(late == 1)(enter)
    for t in range(2, 5):
        layer_one(t, M1)
    for load in loads[3:]:
        load.wait()
    pw_copy.start()
    layer_two([4], M2, True)
    layer_two([6], M2, True)
    layer_two([8], M2, False)
    pl.when(late == 0)(enter)

    def receive(k, buf):
        pl.when(receives[k])(halos[k].wait_recv)

        @pl.when(jnp.logical_not(receives[k]))
        def _():
            buf[...] = jnp.zeros_like(buf)

    flags[me] = flag_ref[...]
    own = out_ref.shape[0]
    places = n * cap
    bits = n.bit_length() - 1
    cap_bits = cap.bit_length() - 1
    shift = shift_ref[0]

    def near_flags(i, c):
        source = lax.rem(me + n - i, n)
        flag_copy(i, source).wait()
        return c + flags[source]

    def far_flags(i, c):
        flag_copy(i, lax.rem(me + n - i, n)).wait()
        return c

    def row_copy(pr, i, source):
        return pltpu.make_async_remote_copy(
            src_ref=sendbuf.at[pr, lax.rem(me + i, n)], dst_ref=got.at[pr, source],
            send_sem=row_send.at[pr, i], recv_sem=row_recv.at[pr, i],
            device_id=(lax.rem(me + i, n), mq), device_id_type=MESH,
        )

    def deal(pr, first):
        spot = lax.broadcasted_iota(jnp.int32, (places, 1), 0)
        upper = jnp.where(
            lax.broadcasted_iota(jnp.int32, (64, 64), 0) < lax.broadcasted_iota(jnp.int32, (64, 64), 1),
            1.0, 0.0,
        ).astype(BF16)
        row = flag_ref[pr : pr + 1].astype(F32)
        within = dot(jnp.broadcast_to(row, (16, 64)).astype(BF16), upper)[0:1]
        rank = jnp.where(row > 0.5, within, -1.0).astype(jnp.int32)
        wanted = (((spot >> cap_bits) - shift - first) & (n - 1)) + n * (spot & (cap - 1))
        pick = jnp.where(rank == wanted, 1.0, 0.0).astype(BF16)
        features = jnp.concatenate(
            [
                s3[h, 2 * pr + a, pl.ds(b, 64, stride=2), :].astype(BF16)
                for a in range(2) for b in range(2) for h in range(2)
            ],
            axis=1,
        )
        rows = dot(pick, features)
        sendbuf[pr] = rows.reshape(n, cap, rows.shape[1]).astype(BF16)

        def send_rows(i, c):
            row_copy(pr, i, me).start()
            return c

        lax.fori_loop(1, n, send_rows, 0)
        got[pr, me] = sendbuf[pr, me]

    receive(1, left)
    for c in range(3):
        slab[24 * c : 24 * c + 24, 0:128] = left[c, 8:32].astype(F32)
    fill_a1(1, 16)
    for t in range(2, 5):
        layer_one(t, 16)
    layer_two([4, 6], 8, True)
    layer_two([8], 8, False)
    layer_three([2, 3], M3)
    near = lax.fori_loop(
        1 + late * me, me + 1 + late * (n - me - 1), near_flags, jnp.zeros(flag_ref.shape, jnp.int32)
    )
    near = jnp.sum(near.astype(F32))
    mine = [jnp.sum(flag_ref[pr : pr + 1].astype(F32), axis=1, keepdims=True) for pr in range(2)]
    start = jnp.where(late == 1, n * own - near - mine[0] - mine[1], near + jnp.zeros((1, 1), F32))
    deal(1, (start + mine[0]).astype(jnp.int32))

    receive(0, top)
    receive(2, corner)
    for c in range(3):
        slab[24 * c : 24 * c + 8, 128:1152] = top[c].astype(F32)
        slab[24 * c : 24 * c + 8, 0:128] = corner[c].astype(F32)
        slab[24 * c + 8 : 24 * c + 24, 128:1152] = img_ref[c, 0:16].astype(F32)
        slab[24 * c + 8 : 24 * c + 24, 0:128] = left[c, 0:16].astype(F32)
    fill_a1(9, M1)
    for t in range(2):
        layer_one(t, M1)
    layer_two([0], M2, True)
    layer_two([2], M2, True)
    layer_three([0, 1], M3)
    deal(0, start.astype(jnp.int32))

    lax.fori_loop(me + 1 - late * me, n - late * (n - me - 1), far_flags, 0)
    src_of = lax.broadcasted_iota(jnp.int32, (n, places), 1) >> cap_bits
    src_at = lax.broadcasted_iota(jnp.int32, (n, places), 0)
    same = jnp.where(src_at == src_of, 1.0, 0.0).astype(BF16)
    earlier = jnp.where(src_at < src_of, 1.0, 0.0).astype(BF16)
    turn = lax.broadcasted_iota(jnp.int32, (1, places), 1) & (cap - 1)
    slots = lax.broadcasted_iota(jnp.int32, (own, places), 0)
    counts = [
        dot_nt(jnp.ones((8, 64), BF16), flags[:, pr, :].astype(F32).astype(BF16)).astype(BF16)
        for pr in range(2)
    ]
    count_l = [dot(part, same)[0:1].astype(jnp.int32) for part in counts]
    start_l = dot(counts[0], earlier)[0:1] + dot(counts[1], earlier)[0:1]
    start_l = start_l.astype(jnp.int32)
    place = []
    for pr in range(2):
        rank_l = ((me - shift - start_l) & (n - 1)) + n * turn
        slot_l = jnp.where(rank_l < count_l[pr], (start_l + rank_l) >> bits, -1)
        place.append(jnp.where(slots == slot_l, 1.0, 0.0).astype(BF16))
        start_l = start_l + count_l[pr]
    filled = jnp.sum(place[0].astype(F32), axis=1, keepdims=True)
    filled = filled + jnp.sum(place[1].astype(F32), axis=1, keepdims=True)
    width = got.shape[3]
    out_ref[:, width:] = jnp.broadcast_to(filled, (own, 128)).astype(BF16)

    placed = None
    for pr in (1, 0):

        def wait_rows(i, c, pr=pr):
            row_copy(pr, i, lax.rem(me + n - i, n)).wait()
            return c

        lax.fori_loop(1, n, wait_rows, 0)
        rows = got[pr].astype(F32).reshape(places, width).astype(BF16)
        part = dot(place[pr], rows)
        placed = part if placed is None else placed + part
    out_ref[:, :width] = placed.astype(BF16)
    for halo, sent in zip(halos, sends):
        pl.when(sent)(halo.wait_send)
    pw_copy.wait()


def project(dealt_ref, pw_ref, pb_ref, out_ref):
    width = pw_ref.shape[0] * pw_ref.shape[1]
    filled = dealt_ref[:, width:].astype(F32)
    filled = jnp.concatenate([filled, filled], axis=1)
    for t in range(6):
        cut = slice(256 * t, 256 * t + 256)
        summed = None
        for k in range(4):
            part = dot(dealt_ref[:, 256 * k : 256 * k + 256], pw_ref[k, :, cut])
            summed = part if summed is None else summed + part
        bias = jnp.concatenate([pb_ref[2 * t : 2 * t + 1], pb_ref[2 * t + 1 : 2 * t + 2]], axis=1)
        out_ref[:, cut] = jnp.where(filled > 0.5, summed + bias, 0.0).astype(BF16)


def local(n, n_seq, slide_image, keep_flags, owner_shift, weight_one, offset_one, weight_two,
          offset_two, weight_three, offset_three, patch_weight, patch_offset):
    patches = keep_flags.size
    embed = patch_weight.shape[2]
    cap = 8 * -(-(-(-keep_flags.shape[1] // n)) // 8)
    width = patch_weight.shape[0] * patch_weight.shape[1]
    arrays = (
        slide_image, keep_flags, weight_one.transpose(0, 2, 1), offset_one[None],
        weight_two.transpose(0, 2, 1), offset_two[None], weight_three, offset_three[None],
    )
    own = patches // 2
    vmem = pl.BlockSpec(memory_space=pltpu.VMEM)
    anywhere = pl.BlockSpec(memory_space=pltpu.HBM)
    dma = pltpu.SemaphoreType.DMA
    dealt, pw = pl.pallas_call(
        functools.partial(kernel, n, n_seq, cap),
        name="stem_and_deal",
        out_shape=(
            pltpu.VMEM((own, width + 128), BF16),
            pltpu.VMEM(patch_weight.shape, BF16),
        ),
        in_specs=[pl.BlockSpec(memory_space=pltpu.SMEM)] + [anywhere] * 9,
        out_specs=(vmem, pl.BlockSpec(memory_space=pltpu.VMEM)),
        scratch_shapes=[
            *(pltpu.VMEM(x.shape, x.dtype) for x in arrays),
            pltpu.VMEM((3, 8, 1024), BF16),
            pltpu.VMEM((3, 32, 128), BF16),
            pltpu.VMEM((3, 8, 128), BF16),
            pltpu.VMEM((n,) + keep_flags.shape, jnp.int32),
            pltpu.VMEM((3, 3, 80, 128), F32),
            pltpu.VMEM((72, 1152), F32),
            pltpu.VMEM((1280, 128), F32),
            pltpu.VMEM((M1, 256), BF16),
            pltpu.VMEM((256, 768), BF16),
            pltpu.VMEM((10, 560, 128), F32),
            pltpu.VMEM((9, M2, 128), F32),
            pltpu.VMEM((2, 4, M3, 128), F32),
            pltpu.VMEM((2, n, cap, width), BF16),
            pltpu.VMEM((2, n, cap, width), BF16),
            dma((3,)), dma((3,)), dma((n,)), dma((n,)), dma((2, n)), dma((2, n)), dma((8,)), dma(()),
        ],
        compiler_params=pltpu.CompilerParams(
            collective_id=0, has_side_effects=True, vmem_limit_bytes=VMEM1
        ),
    )(
        owner_shift, *arrays, patch_weight,
    )
    placed = pl.pallas_call(
        project,
        name="project",
        out_shape=jax.ShapeDtypeStruct((own, embed), BF16),
        in_specs=[vmem] * 3,
        out_specs=vmem,
        compiler_params=pltpu.CompilerParams(vmem_limit_bytes=16 << 20),
    )(dealt, pw, patch_offset.reshape(-1, 128))
    return placed[None]


def solution(mesh):
    args = (P(None, "strip", "seq"), P("strip", "seq"), P("seq")) + (P(),) * 8
    return jax.shard_map(
        functools.partial(local, mesh.shape["strip"], mesh.shape["seq"]),
        mesh=mesh, in_specs=args, out_specs=P("seq", "strip", None), check_vma=False,
    )
```

```python
import functools

import jax
import jax.numpy as jnp
from jax import lax
from jax.experimental import pallas as pl
from jax.experimental.pallas import tpu as pltpu
from jax.sharding import PartitionSpec as P

MESH = pl.DeviceIdType.MESH
F32 = jnp.float32
BF16 = jnp.bfloat16

M1 = 528
M2 = 272
M3 = 128
VMEM1 = 60000000


def gelu(x):
    return 0.5 * x * (1.0 + lax.erf(x * 0.7071067811865476))


def dot(a, b):
    return jnp.dot(a, b, preferred_element_type=F32)


def dot_nt(a, b):
    return lax.dot_general(a, b, (((1,), (1,)), ((), ())), preferred_element_type=F32)


def kernel(
    n, n_seq, cap,
    shift_ref, img_hbm, flag_hbm, w1_hbm, b1_hbm, w2_hbm, b2_hbm, w3_hbm, b3_hbm, pw_hbm,
    out_ref, pw_out,
    img_ref, flag_ref, w1_ref, b1_ref, w2_ref, b2_ref, w3_ref, b3_ref, top, left, corner, flags, band, slab, slab_t, a1, k1, s1, s2, s3, sendbuf, got,
    halo_send, halo_recv, flag_send, flag_recv, row_send, row_recv, load_sem, pw_sem,
):
    me = lax.axis_index("strip")
    mq = lax.axis_index("seq")
    half = n // 2
    late = me // half
    down, up = lax.rem(me + 1, n), lax.rem(me + n - 1, n)
    right, leftward = lax.rem(mq + 1, n_seq), lax.rem(mq + n_seq - 1, n_seq)

    loads = [
        pltpu.make_async_copy(src, dst, load_sem.at[k])
        for k, (src, dst) in enumerate(
            (
                (w1_hbm, w1_ref), (img_hbm, img_ref), (b1_hbm, b1_ref), (w2_hbm, w2_ref),
                (b2_hbm, b2_ref), (w3_hbm, w3_ref), (b3_hbm, b3_ref), (flag_hbm, flag_ref),
            )
        )
    ]
    barrier = pltpu.get_barrier_semaphore()

    def greet(i, c):
        pl.semaphore_signal(barrier, inc=1, device_id=(lax.rem(me + i, n), mq), device_id_type=MESH)
        return c

    for load in loads[:2]:
        load.start()
    for where in ((me, right), (me, leftward), (down, right), (up, leftward)):
        pl.semaphore_signal(barrier, inc=1, device_id=where, device_id_type=MESH)
    lax.fori_loop(1, n, greet, 0)
    for load in loads[2:]:
        load.start()

    pw_copy = pltpu.make_async_copy(pw_hbm, pw_out, pw_sem)

    def flag_copy(i, source):
        return pltpu.make_async_remote_copy(
            src_ref=flag_hbm, dst_ref=flags.at[source],
            send_sem=flag_send.at[i], recv_sem=flag_recv.at[i],
            device_id=(lax.rem(me + i, n), mq), device_id_type=MESH,
        )

    halos = [
        pltpu.make_async_remote_copy(
            src_ref=src, dst_ref=dst, send_sem=halo_send.at[k], recv_sem=halo_recv.at[k],
            device_id=where, device_id_type=MESH,
        )
        for k, (src, dst, where) in enumerate(
            (
                (img_ref.at[:, 24:32, :], top, (down, mq)),
                (img_ref.at[:, :, 896:1024], left, (me, right)),
                (img_ref.at[:, 24:32, 896:1024], corner, (down, right)),
            )
        )
    ]
    inner_row = me > 0
    inner_col = mq > 0
    to_down, to_right = me < n - 1, mq < n_seq - 1
    sends = (to_down, to_right, jnp.logical_and(to_down, to_right))
    receives = (inner_row, inner_col, jnp.logical_and(inner_row, inner_col))

    def send_flags(i, c):
        flag_copy(i, me).start()
        return c

    def enter():
        pl.semaphore_wait(barrier, n - 1 + 4)
        for halo, sent in zip(halos, sends):
            pl.when(sent)(halo.start)
        lax.fori_loop(1, n, send_flags, 0)

    loads[0].wait()
    low = lax.broadcasted_iota(jnp.int32, (8, 128), 0)
    low_lane = lax.broadcasted_iota(jnp.int32, (8, 128), 1)
    tap = low - 1 - 2 * jnp.where(low_lane >= 64, 1, 0)
    band[...] = jnp.zeros_like(band)
    for dx in range(3):
        tap_w = [w1_ref[3 * dy + dx].astype(F32) for dy in range(3)]
        tap_w = [jnp.concatenate([w, w], axis=1) for w in tap_w]
        for c in range(3):
            block = jnp.zeros((8, 128), F32)
            for dy in range(3):
                block = jnp.where(tap == dy, jnp.broadcast_to(tap_w[dy][c : c + 1], (8, 128)), block)
            band[dx, c, 40:48, :] = block
    for q in range(6):
        parts = [band[dx, c, 40 - 4 * q : 64 - 4 * q, :] for dx in range(3) for c in range(3)]
        parts = jnp.concatenate(parts + [jnp.zeros((40, 128), F32)], axis=0)
        k1[:, 128 * q : 128 * q + 128] = parts.astype(BF16)

    slab[:, 0:128] = jnp.zeros((72, 128), F32)
    slab_t[...] = jnp.zeros_like(slab_t)
    loads[1].wait()
    for c in range(3):
        slab[24 * c : 24 * c + 24, 128:1152] = img_ref[c, 8:32].astype(F32)

    def fill_a1(tiles, rows):
        for t in range(tiles):
            slab_t[128 * t : 128 * t + 128, 0:72] = slab[:, 128 * t : 128 * t + 128].T
        one, two, three = [slab_t[pl.ds(119 + dx, rows, stride=2), :] for dx in range(3)]
        two = pltpu.roll(two, 72, axis=1)
        three = pltpu.roll(three, 16, axis=1)
        lane = lax.broadcasted_iota(jnp.int32, (rows, 128), 1)
        a1[:rows, 0:128] = jnp.where(lane < 72, one, two).astype(BF16)
        a1[:rows, 128:256] = jnp.where(lane < 16, two, three).astype(BF16)

    fill_a1(9, M1)
    loads[2].wait()
    b1 = jnp.concatenate([b1_ref[...]] * 4, axis=1)

    def layer_one(t, rows):
        act = gelu(dot(a1[:rows], k1[:, 256 * (t % 2 + t // 4 * 2) : 256 * (t % 2 + t // 4 * 2) + 256]) + b1)
        if t < 2 or rows < M1:
            sub1 = lax.broadcasted_iota(jnp.int32, (rows, 256), 0)
            ok = jnp.logical_or(inner_col, sub1 >= 4)
            if t == 0:
                lane1 = lax.broadcasted_iota(jnp.int32, (rows, 256), 1)
                ok = jnp.logical_and(ok, jnp.logical_or(inner_row, lane1 >= 192))
            act = jnp.where(ok, act, 0.0)
        s1[2 * t, :rows] = act[:, :128]
        s1[2 * t + 1, :rows] = act[:, 128:]

    none = jnp.zeros((64, 128), BF16)

    def tap2(dy, dx):
        return none if dy is None else w2_ref[3 * dy + dx]

    def layer_two(where, rows, pair):
        tiles = (0, 1, 2) if pair else (0, 1)
        order = [(h, dx) for dx in range(3) for h in (0, 1)] + [(2, dx) for dx in range(3) if pair]
        a = jnp.concatenate(
            [
                jnp.concatenate(
                    [s1[r + h, pl.ds(1 + dx, rows, stride=2), :] for r in where], axis=0
                ).astype(BF16)
                for h, dx in order
            ],
            axis=1,
        )
        first = {0: (0, 1), 1: (2, None), 2: (None, None)}
        second = {0: (None, None), 1: (0, 1), 2: (2, None)}
        w2 = []
        for h, dx in order:
            for part in range(2):
                row = [tap2(first[h][part], dx)]
                if pair:
                    row.append(tap2(second[h][part], dx))
                w2.append(jnp.concatenate(row, axis=1))
        summed = dot(a, jnp.concatenate(w2, axis=0))
        bias = jnp.concatenate([b2_ref[...]] * (2 if pair else 1), axis=1)
        act = gelu(summed + bias)
        sub2 = lax.broadcasted_iota(jnp.int32, (rows, 128), 0)
        col_ok2 = jnp.logical_or(inner_col, sub2 >= 1)
        for k, r in enumerate(where):
            for more in range(2 if pair else 1):
                one = act[rows * k : rows * k + rows, 128 * more : 128 * more + 128]
                if r < 4 or rows < M2:
                    ok = jnp.logical_and(col_ok2, inner_row) if r + more == 0 else col_ok2
                    one = jnp.where(ok, one, 0.0)
                s2[r + more, :rows] = one

    def layer_three(where, rows):
        taps = [(dy, dx) for dy in range(3) for dx in range(3)]
        a = jnp.concatenate(
            [
                jnp.concatenate(
                    [s2[2 * r + dy, pl.ds(dx, rows, stride=2), :] for r in where], axis=0
                ).astype(BF16)
                for dy, dx in taps
            ],
            axis=1,
        )
        w3 = jnp.concatenate([w3_ref[3 * dy + dx] for dy, dx in taps], axis=1)
        act = gelu(dot_nt(a, w3) + b3_ref[...])
        for k, r in enumerate(where):
            s3[0, r, :rows] = act[rows * k : rows * k + rows, :128]
            s3[1, r, :rows] = act[rows * k : rows * k + rows, 128:]

    pl.when(late == 1)(enter)
    for t in range(2, 5):
        layer_one(t, M1)
    for load in loads[3:]:
        load.wait()
    pw_copy.start()
    layer_two([4], M2, True)
    layer_two([6], M2, True)
    layer_two([8], M2, False)
    pl.when(late == 0)(enter)

    def receive(k, buf):
        pl.when(receives[k])(halos[k].wait_recv)

        @pl.when(jnp.logical_not(receives[k]))
        def _():
            buf[...] = jnp.zeros_like(buf)

    flags[me] = flag_ref[...]
    own = out_ref.shape[0]
    places = n * cap
    bits = n.bit_length() - 1
    cap_bits = cap.bit_length() - 1
    shift = shift_ref[0]

    def near_flags(i, c):
        source = lax.rem(me + n - i, n)
        flag_copy(i, source).wait()
        return c + flags[source]

    def far_flags(i, c):
        flag_copy(i, lax.rem(me + n - i, n)).wait()
        return c

    def row_copy(pr, i, source):
        return pltpu.make_async_remote_copy(
            src_ref=sendbuf.at[pr, lax.rem(me + i, n)], dst_ref=got.at[pr, source],
            send_sem=row_send.at[pr, i], recv_sem=row_recv.at[pr, i],
            device_id=(lax.rem(me + i, n), mq), device_id_type=MESH,
        )

    def deal(pr, first):
        spot = lax.broadcasted_iota(jnp.int32, (places, 1), 0)
        upper = jnp.where(
            lax.broadcasted_iota(jnp.int32, (64, 64), 0) < lax.broadcasted_iota(jnp.int32, (64, 64), 1),
            1.0, 0.0,
        ).astype(BF16)
        row = flag_ref[pr : pr + 1].astype(F32)
        within = dot(jnp.broadcast_to(row, (16, 64)).astype(BF16), upper)[0:1]
        rank = jnp.where(row > 0.5, within, -1.0).astype(jnp.int32)
        wanted = (((spot >> cap_bits) - shift - first) & (n - 1)) + n * (spot & (cap - 1))
        pick = jnp.where(rank == wanted, 1.0, 0.0).astype(BF16)
        features = jnp.concatenate(
            [
                s3[h, 2 * pr + a, pl.ds(b, 64, stride=2), :].astype(BF16)
                for a in range(2) for b in range(2) for h in range(2)
            ],
            axis=1,
        )
        rows = dot(pick, features)
        sendbuf[pr] = rows.reshape(n, cap, rows.shape[1]).astype(BF16)

        def send_rows(i, c):
            row_copy(pr, i, me).start()
            return c

        lax.fori_loop(1, n, send_rows, 0)
        got[pr, me] = sendbuf[pr, me]

    receive(1, left)
    for c in range(3):
        slab[24 * c : 24 * c + 24, 0:128] = left[c, 8:32].astype(F32)
    fill_a1(1, 16)
    for t in range(2, 5):
        layer_one(t, 16)
    layer_two([4, 6], 8, True)
    layer_two([8], 8, False)
    layer_three([2, 3], M3)
    near = lax.fori_loop(
        1 + late * me, me + 1 + late * (n - me - 1), near_flags, jnp.zeros(flag_ref.shape, jnp.int32)
    )
    near = jnp.sum(near.astype(F32))
    mine = [jnp.sum(flag_ref[pr : pr + 1].astype(F32), axis=1, keepdims=True) for pr in range(2)]
    start = jnp.where(late == 1, n * own - near - mine[0] - mine[1], near + jnp.zeros((1, 1), F32))
    deal(1, (start + mine[0]).astype(jnp.int32))

    receive(0, top)
    receive(2, corner)
    for c in range(3):
        slab[24 * c : 24 * c + 8, 128:1152] = top[c].astype(F32)
        slab[24 * c : 24 * c + 8, 0:128] = corner[c].astype(F32)
        slab[24 * c + 8 : 24 * c + 24, 128:1152] = img_ref[c, 0:16].astype(F32)
        slab[24 * c + 8 : 24 * c + 24, 0:128] = left[c, 0:16].astype(F32)
    fill_a1(9, M1)
    for t in range(2):
        layer_one(t, M1)
    layer_two([0], M2, True)
    layer_two([2], M2, True)
    layer_three([0, 1], M3)
    deal(0, start.astype(jnp.int32))

    lax.fori_loop(me + 1 - late * me, n - late * (n - me - 1), far_flags, 0)
    src_of = lax.broadcasted_iota(jnp.int32, (n, places), 1) >> cap_bits
    src_at = lax.broadcasted_iota(jnp.int32, (n, places), 0)
    same = jnp.where(src_at == src_of, 1.0, 0.0).astype(BF16)
    earlier = jnp.where(src_at < src_of, 1.0, 0.0).astype(BF16)
    turn = lax.broadcasted_iota(jnp.int32, (1, places), 1) & (cap - 1)
    slots = lax.broadcasted_iota(jnp.int32, (own, places), 0)
    counts = [
        dot_nt(jnp.ones((8, 64), BF16), flags[:, pr, :].astype(F32).astype(BF16)).astype(BF16)
        for pr in range(2)
    ]
    count_l = [dot(part, same)[0:1].astype(jnp.int32) for part in counts]
    start_l = dot(counts[0], earlier)[0:1] + dot(counts[1], earlier)[0:1]
    start_l = start_l.astype(jnp.int32)
    place = []
    for pr in range(2):
        rank_l = ((me - shift - start_l) & (n - 1)) + n * turn
        slot_l = jnp.where(rank_l < count_l[pr], (start_l + rank_l) >> bits, -1)
        place.append(jnp.where(slots == slot_l, 1.0, 0.0).astype(BF16))
        start_l = start_l + count_l[pr]
    filled = jnp.sum(place[0].astype(F32), axis=1, keepdims=True)
    filled = filled + jnp.sum(place[1].astype(F32), axis=1, keepdims=True)
    width = got.shape[3]
    out_ref[:, width:] = jnp.broadcast_to(filled, (own, 128)).astype(BF16)

    placed = None
    for pr in (1, 0):

        def wait_rows(i, c, pr=pr):
            row_copy(pr, i, lax.rem(me + n - i, n)).wait()
            return c

        lax.fori_loop(1, n, wait_rows, 0)
        rows = got[pr].astype(F32).reshape(places, width).astype(BF16)
        part = dot(place[pr], rows)
        placed = part if placed is None else placed + part
    out_ref[:, :width] = placed.astype(BF16)
    for halo, sent in zip(halos, sends):
        pl.when(sent)(halo.wait_send)
    pw_copy.wait()


def project(dealt_ref, pw_ref, pb_ref, out_ref):
    width = pw_ref.shape[0] * pw_ref.shape[1]
    filled = dealt_ref[:, width:].astype(F32)
    filled = jnp.concatenate([filled, filled], axis=1)
    for t in range(6):
        cut = slice(256 * t, 256 * t + 256)
        weight = jnp.concatenate([pw_ref[k, :, cut] for k in range(4)], axis=0)
        summed = dot(dealt_ref[:, :width], weight)
        bias = jnp.concatenate([pb_ref[2 * t : 2 * t + 1], pb_ref[2 * t + 1 : 2 * t + 2]], axis=1)
        out_ref[:, cut] = jnp.where(filled > 0.5, summed + bias, 0.0).astype(BF16)


def local(n, n_seq, slide_image, keep_flags, owner_shift, weight_one, offset_one, weight_two,
          offset_two, weight_three, offset_three, patch_weight, patch_offset):
    patches = keep_flags.size
    embed = patch_weight.shape[2]
    cap = 8 * -(-(-(-keep_flags.shape[1] // n)) // 8)
    width = patch_weight.shape[0] * patch_weight.shape[1]
    arrays = (
        slide_image, keep_flags, weight_one.transpose(0, 2, 1), offset_one[None],
        weight_two.transpose(0, 2, 1), offset_two[None], weight_three, offset_three[None],
    )
    own = patches // 2
    vmem = pl.BlockSpec(memory_space=pltpu.VMEM)
    anywhere = pl.BlockSpec(memory_space=pltpu.HBM)
    dma = pltpu.SemaphoreType.DMA
    dealt, pw = pl.pallas_call(
        functools.partial(kernel, n, n_seq, cap),
        name="stem_and_deal",
        out_shape=(
            pltpu.VMEM((own, width + 128), BF16),
            pltpu.VMEM(patch_weight.shape, BF16),
        ),
        in_specs=[pl.BlockSpec(memory_space=pltpu.SMEM)] + [anywhere] * 9,
        out_specs=(vmem, pl.BlockSpec(memory_space=pltpu.VMEM)),
        scratch_shapes=[
            *(pltpu.VMEM(x.shape, x.dtype) for x in arrays),
            pltpu.VMEM((3, 8, 1024), BF16),
            pltpu.VMEM((3, 32, 128), BF16),
            pltpu.VMEM((3, 8, 128), BF16),
            pltpu.VMEM((n,) + keep_flags.shape, jnp.int32),
            pltpu.VMEM((3, 3, 80, 128), F32),
            pltpu.VMEM((72, 1152), F32),
            pltpu.VMEM((1280, 128), F32),
            pltpu.VMEM((M1, 256), BF16),
            pltpu.VMEM((256, 768), BF16),
            pltpu.VMEM((10, 560, 128), F32),
            pltpu.VMEM((9, M2, 128), F32),
            pltpu.VMEM((2, 4, M3, 128), F32),
            pltpu.VMEM((2, n, cap, width), BF16),
            pltpu.VMEM((2, n, cap, width), BF16),
            dma((3,)), dma((3,)), dma((n,)), dma((n,)), dma((2, n)), dma((2, n)), dma((8,)), dma(()),
        ],
        compiler_params=pltpu.CompilerParams(
            collective_id=0, has_side_effects=True, vmem_limit_bytes=VMEM1
        ),
    )(
        owner_shift, *arrays, patch_weight,
    )
    placed = pl.pallas_call(
        project,
        name="project",
        out_shape=jax.ShapeDtypeStruct((own, embed), BF16),
        in_specs=[vmem] * 3,
        out_specs=vmem,
        compiler_params=pltpu.CompilerParams(vmem_limit_bytes=16 << 20),
    )(dealt, pw, patch_offset.reshape(-1, 128))
    return placed[None]


def solution(mesh):
    args = (P(None, "strip", "seq"), P("strip", "seq"), P("seq")) + (P(),) * 8
    return jax.shard_map(
        functools.partial(local, mesh.shape["strip"], mesh.shape["seq"]),
        mesh=mesh, in_specs=args, out_specs=P("seq", "strip", None), check_vma=False,
    )
```

```python
import functools

import jax
import jax.numpy as jnp
from jax import lax
from jax.experimental import pallas as pl
from jax.experimental.pallas import tpu as pltpu
from jax.sharding import PartitionSpec as P

MESH = pl.DeviceIdType.MESH
F32 = jnp.float32
BF16 = jnp.bfloat16

M1 = 528
M2 = 272
M3 = 128
VMEM1 = 60000000


def gelu(x):
    return 0.5 * x * (1.0 + lax.erf(x * 0.7071067811865476))


def dot(a, b):
    return jnp.dot(a, b, preferred_element_type=F32)


def dot_nt(a, b):
    return lax.dot_general(a, b, (((1,), (1,)), ((), ())), preferred_element_type=F32)


def kernel(
    n, n_seq, cap,
    shift_ref, img_hbm, flag_hbm, w1_hbm, b1_hbm, w2_hbm, b2_hbm, w3_hbm, b3_hbm, pw_hbm,
    out_ref, pw_out,
    img_ref, flag_ref, w1_ref, b1_ref, w2_ref, b2_ref, w3_ref, b3_ref, top, left, corner, flags, band, slab, slab_t, a1, k1, s1, s2, s3, sendbuf, got,
    halo_send, halo_recv, flag_send, flag_recv, row_send, row_recv, load_sem, pw_sem,
):
    me = lax.axis_index("strip")
    mq = lax.axis_index("seq")
    half = n // 2
    late = me // half
    down, up = lax.rem(me + 1, n), lax.rem(me + n - 1, n)
    right, leftward = lax.rem(mq + 1, n_seq), lax.rem(mq + n_seq - 1, n_seq)

    loads = [
        pltpu.make_async_copy(src, dst, load_sem.at[k])
        for k, (src, dst) in enumerate(
            (
                (w1_hbm, w1_ref), (img_hbm, img_ref), (b1_hbm, b1_ref), (w2_hbm, w2_ref),
                (b2_hbm, b2_ref), (w3_hbm, w3_ref), (b3_hbm, b3_ref), (flag_hbm, flag_ref),
            )
        )
    ]
    barrier = pltpu.get_barrier_semaphore()

    def greet(i, c):
        pl.semaphore_signal(barrier, inc=1, device_id=(lax.rem(me + i, n), mq), device_id_type=MESH)
        return c

    for load in loads[:2]:
        load.start()
    for where in ((me, right), (me, leftward), (down, right), (up, leftward)):
        pl.semaphore_signal(barrier, inc=1, device_id=where, device_id_type=MESH)
    lax.fori_loop(1, n, greet, 0)
    for load in loads[2:]:
        load.start()

    pw_copy = pltpu.make_async_copy(pw_hbm, pw_out, pw_sem)

    def flag_copy(i, source):
        return pltpu.make_async_remote_copy(
            src_ref=flag_hbm, dst_ref=flags.at[source],
            send_sem=flag_send.at[i], recv_sem=flag_recv.at[i],
            device_id=(lax.rem(me + i, n), mq), device_id_type=MESH,
        )

    halos = [
        pltpu.make_async_remote_copy(
            src_ref=src, dst_ref=dst, send_sem=halo_send.at[k], recv_sem=halo_recv.at[k],
            device_id=where, device_id_type=MESH,
        )
        for k, (src, dst, where) in enumerate(
            (
                (img_ref.at[:, 24:32, :], top, (down, mq)),
                (img_ref.at[:, :, 896:1024], left, (me, right)),
                (img_ref.at[:, 24:32, 896:1024], corner, (down, right)),
            )
        )
    ]
    inner_row = me > 0
    inner_col = mq > 0
    to_down, to_right = me < n - 1, mq < n_seq - 1
    sends = (to_down, to_right, jnp.logical_and(to_down, to_right))
    receives = (inner_row, inner_col, jnp.logical_and(inner_row, inner_col))

    def send_flags(i, c):
        flag_copy(i, me).start()
        return c

    def enter():
        pl.semaphore_wait(barrier, n - 1 + 4)
        for halo, sent in zip(halos, sends):
            pl.when(sent)(halo.start)
        lax.fori_loop(1, n, send_flags, 0)

    loads[0].wait()
    low = lax.broadcasted_iota(jnp.int32, (8, 128), 0)
    low_lane = lax.broadcasted_iota(jnp.int32, (8, 128), 1)
    tap = low - 1 - 2 * jnp.where(low_lane >= 64, 1, 0)
    band[...] = jnp.zeros_like(band)
    for dx in range(3):
        tap_w = [w1_ref[3 * dy + dx].astype(F32) for dy in range(3)]
        tap_w = [jnp.concatenate([w, w], axis=1) for w in tap_w]
        for c in range(3):
            block = jnp.zeros((8, 128), F32)
            for dy in range(3):
                block = jnp.where(tap == dy, jnp.broadcast_to(tap_w[dy][c : c + 1], (8, 128)), block)
            band[dx, c, 40:48, :] = block
    for q in range(6):
        parts = [band[dx, c, 40 - 4 * q : 64 - 4 * q, :] for dx in range(3) for c in range(3)]
        parts = jnp.concatenate(parts + [jnp.zeros((40, 128), F32)], axis=0)
        k1[:, 128 * q : 128 * q + 128] = parts.astype(BF16)

    slab[:, 0:128] = jnp.zeros((72, 128), F32)
    slab_t[...] = jnp.zeros_like(slab_t)
    loads[1].wait()
    for c in range(3):
        slab[24 * c : 24 * c + 24, 128:1152] = img_ref[c, 8:32].astype(F32)

    def fill_a1(tiles, rows):
        for t in range(tiles):
            slab_t[128 * t : 128 * t + 128, 0:72] = slab[:, 128 * t : 128 * t + 128].T
        one, two, three = [slab_t[pl.ds(119 + dx, rows, stride=2), :] for dx in range(3)]
        two = pltpu.roll(two, 72, axis=1)
        three = pltpu.roll(three, 16, axis=1)
        lane = lax.broadcasted_iota(jnp.int32, (rows, 128), 1)
        a1[:rows, 0:128] = jnp.where(lane < 72, one, two).astype(BF16)
        a1[:rows, 128:256] = jnp.where(lane < 16, two, three).astype(BF16)

    fill_a1(9, M1)
    loads[2].wait()
    b1 = jnp.concatenate([b1_ref[...]] * 4, axis=1)

    def layer_one(t, rows):
        act = gelu(dot(a1[:rows], k1[:, 256 * (t % 2 + t // 4 * 2) : 256 * (t % 2 + t // 4 * 2) + 256]) + b1)
        if t < 2 or rows < M1:
            sub1 = lax.broadcasted_iota(jnp.int32, (rows, 256), 0)
            ok = jnp.logical_or(inner_col, sub1 >= 4)
            if t == 0:
                lane1 = lax.broadcasted_iota(jnp.int32, (rows, 256), 1)
                ok = jnp.logical_and(ok, jnp.logical_or(inner_row, lane1 >= 192))
            act = jnp.where(ok, act, 0.0)
        s1[2 * t, :rows] = act[:, :128]
        s1[2 * t + 1, :rows] = act[:, 128:]

    none = jnp.zeros((64, 128), BF16)

    def tap2(dy, dx):
        return none if dy is None else w2_ref[3 * dy + dx]

    def layer_two(where, rows, pair):
        tiles = (0, 1, 2) if pair else (0, 1)
        order = [(h, dx) for dx in range(3) for h in (0, 1)] + [(2, dx) for dx in range(3) if pair]
        a = jnp.concatenate(
            [
                jnp.concatenate(
                    [s1[r + h, pl.ds(1 + dx, rows, stride=2), :] for r in where], axis=0
                ).astype(BF16)
                for h, dx in order
            ],
            axis=1,
        )
        first = {0: (0, 1), 1: (2, None), 2: (None, None)}
        second = {0: (None, None), 1: (0, 1), 2: (2, None)}
        w2 = []
        for h, dx in order:
            for part in range(2):
                row = [tap2(first[h][part], dx)]
                if pair:
                    row.append(tap2(second[h][part], dx))
                w2.append(jnp.concatenate(row, axis=1))
        summed = dot(a, jnp.concatenate(w2, axis=0))
        bias = jnp.concatenate([b2_ref[...]] * (2 if pair else 1), axis=1)
        act = gelu(summed + bias)
        sub2 = lax.broadcasted_iota(jnp.int32, (rows, 128), 0)
        col_ok2 = jnp.logical_or(inner_col, sub2 >= 1)
        for k, r in enumerate(where):
            for more in range(2 if pair else 1):
                one = act[rows * k : rows * k + rows, 128 * more : 128 * more + 128]
                if r < 4 or rows < M2:
                    ok = jnp.logical_and(col_ok2, inner_row) if r + more == 0 else col_ok2
                    one = jnp.where(ok, one, 0.0)
                s2[r + more, :rows] = one

    def layer_three(where, rows):
        taps = [(dy, dx) for dy in range(3) for dx in range(3)]
        a = jnp.concatenate(
            [
                jnp.concatenate(
                    [s2[2 * r + dy, pl.ds(dx, rows, stride=2), :] for r in where], axis=0
                ).astype(BF16)
                for dy, dx in taps
            ],
            axis=1,
        )
        w3 = jnp.concatenate([w3_ref[3 * dy + dx] for dy, dx in taps], axis=1)
        act = gelu(dot_nt(a, w3) + b3_ref[...])
        for k, r in enumerate(where):
            s3[0, r, :rows] = act[rows * k : rows * k + rows, :128]
            s3[1, r, :rows] = act[rows * k : rows * k + rows, 128:]

    pl.when(late == 1)(enter)
    for t in range(2, 5):
        layer_one(t, M1)
    for load in loads[3:]:
        load.wait()
    pw_copy.start()
    layer_two([4], M2, True)
    layer_two([6], M2, True)
    layer_two([8], M2, False)
    pl.when(late == 0)(enter)

    def receive(k, buf):
        pl.when(receives[k])(halos[k].wait_recv)

        @pl.when(jnp.logical_not(receives[k]))
        def _():
            buf[...] = jnp.zeros_like(buf)

    flags[me] = flag_ref[...]
    own = out_ref.shape[0]
    places = n * cap
    bits = n.bit_length() - 1
    cap_bits = cap.bit_length() - 1
    shift = shift_ref[0]

    def near_flags(i, c):
        source = lax.rem(me + n - i, n)
        flag_copy(i, source).wait()
        return c + flags[source]

    def far_flags(i, c):
        flag_copy(i, lax.rem(me + n - i, n)).wait()
        return c

    def row_copy(pr, i, source):
        return pltpu.make_async_remote_copy(
            src_ref=sendbuf.at[pr, lax.rem(me + i, n)], dst_ref=got.at[pr, source],
            send_sem=row_send.at[pr, i], recv_sem=row_recv.at[pr, i],
            device_id=(lax.rem(me + i, n), mq), device_id_type=MESH,
        )

    def deal(pr, first):
        spot = lax.broadcasted_iota(jnp.int32, (places, 1), 0)
        upper = jnp.where(
            lax.broadcasted_iota(jnp.int32, (64, 64), 0) < lax.broadcasted_iota(jnp.int32, (64, 64), 1),
            1.0, 0.0,
        ).astype(BF16)
        row = flag_ref[pr : pr + 1].astype(F32)
        within = dot(jnp.broadcast_to(row, (16, 64)).astype(BF16), upper)[0:1]
        rank = jnp.where(row > 0.5, within, -1.0).astype(jnp.int32)
        wanted = (((spot >> cap_bits) - shift - first) & (n - 1)) + n * (spot & (cap - 1))
        pick = jnp.where(rank == wanted, 1.0, 0.0).astype(BF16)
        features = jnp.concatenate(
            [
                s3[h, 2 * pr + a, pl.ds(b, 64, stride=2), :].astype(BF16)
                for a in range(2) for b in range(2) for h in range(2)
            ],
            axis=1,
        )
        rows = dot(pick, features)
        sendbuf[pr] = rows.reshape(n, cap, rows.shape[1]).astype(BF16)

        def send_rows(i, c):
            row_copy(pr, late * i + (1 - late) * (n - i), me).start()
            return c

        lax.fori_loop(1, n, send_rows, 0)
        got[pr, me] = sendbuf[pr, me]

    receive(1, left)
    for c in range(3):
        slab[24 * c : 24 * c + 24, 0:128] = left[c, 8:32].astype(F32)
    fill_a1(1, 16)
    for t in range(2, 5):
        layer_one(t, 16)
    layer_two([4, 6], 8, True)
    layer_two([8], 8, False)
    layer_three([2, 3], M3)
    near = lax.fori_loop(
        1 + late * me, me + 1 + late * (n - me - 1), near_flags, jnp.zeros(flag_ref.shape, jnp.int32)
    )
    near = jnp.sum(near.astype(F32))
    mine = [jnp.sum(flag_ref[pr : pr + 1].astype(F32), axis=1, keepdims=True) for pr in range(2)]
    start = jnp.where(late == 1, n * own - near - mine[0] - mine[1], near + jnp.zeros((1, 1), F32))
    deal(1, (start + mine[0]).astype(jnp.int32))

    receive(0, top)
    receive(2, corner)
    for c in range(3):
        slab[24 * c : 24 * c + 8, 128:1152] = top[c].astype(F32)
        slab[24 * c : 24 * c + 8, 0:128] = corner[c].astype(F32)
        slab[24 * c + 8 : 24 * c + 24, 128:1152] = img_ref[c, 0:16].astype(F32)
        slab[24 * c + 8 : 24 * c + 24, 0:128] = left[c, 0:16].astype(F32)
    fill_a1(9, M1)
    for t in range(2):
        layer_one(t, M1)
    layer_two([0], M2, True)
    layer_two([2], M2, True)
    layer_three([0, 1], M3)
    deal(0, start.astype(jnp.int32))

    lax.fori_loop(me + 1 - late * me, n - late * (n - me - 1), far_flags, 0)
    src_of = lax.broadcasted_iota(jnp.int32, (n, places), 1) >> cap_bits
    src_at = lax.broadcasted_iota(jnp.int32, (n, places), 0)
    same = jnp.where(src_at == src_of, 1.0, 0.0).astype(BF16)
    earlier = jnp.where(src_at < src_of, 1.0, 0.0).astype(BF16)
    turn = lax.broadcasted_iota(jnp.int32, (1, places), 1) & (cap - 1)
    slots = lax.broadcasted_iota(jnp.int32, (own, places), 0)
    counts = [
        dot_nt(jnp.ones((8, 64), BF16), flags[:, pr, :].astype(F32).astype(BF16)).astype(BF16)
        for pr in range(2)
    ]
    count_l = [dot(part, same)[0:1].astype(jnp.int32) for part in counts]
    start_l = dot(counts[0], earlier)[0:1] + dot(counts[1], earlier)[0:1]
    start_l = start_l.astype(jnp.int32)
    place = []
    for pr in range(2):
        rank_l = ((me - shift - start_l) & (n - 1)) + n * turn
        slot_l = jnp.where(rank_l < count_l[pr], (start_l + rank_l) >> bits, -1)
        place.append(jnp.where(slots == slot_l, 1.0, 0.0).astype(BF16))
        start_l = start_l + count_l[pr]
    filled = jnp.sum(place[0].astype(F32), axis=1, keepdims=True)
    filled = filled + jnp.sum(place[1].astype(F32), axis=1, keepdims=True)
    width = got.shape[3]
    out_ref[:, width:] = jnp.broadcast_to(filled, (own, 128)).astype(BF16)

    placed = None
    for pr in (1, 0):

        def wait_rows(i, c, pr=pr):
            row_copy(pr, i, lax.rem(me + n - i, n)).wait()
            return c

        lax.fori_loop(1, n, wait_rows, 0)
        rows = got[pr].astype(F32).reshape(places, width).astype(BF16)
        part = dot(place[pr], rows)
        placed = part if placed is None else placed + part
    out_ref[:, :width] = placed.astype(BF16)
    for halo, sent in zip(halos, sends):
        pl.when(sent)(halo.wait_send)
    pw_copy.wait()


def project(dealt_ref, pw_ref, pb_ref, out_ref):
    width = pw_ref.shape[0] * pw_ref.shape[1]
    filled = dealt_ref[:, width:].astype(F32)
    filled = jnp.concatenate([filled, filled], axis=1)
    for t in range(6):
        cut = slice(256 * t, 256 * t + 256)
        weight = jnp.concatenate([pw_ref[k, :, cut] for k in range(4)], axis=0)
        summed = dot(dealt_ref[:, :width], weight)
        bias = jnp.concatenate([pb_ref[2 * t : 2 * t + 1], pb_ref[2 * t + 1 : 2 * t + 2]], axis=1)
        out_ref[:, cut] = jnp.where(filled > 0.5, summed + bias, 0.0).astype(BF16)


def local(n, n_seq, slide_image, keep_flags, owner_shift, weight_one, offset_one, weight_two,
          offset_two, weight_three, offset_three, patch_weight, patch_offset):
    patches = keep_flags.size
    embed = patch_weight.shape[2]
    cap = 8 * -(-(-(-keep_flags.shape[1] // n)) // 8)
    width = patch_weight.shape[0] * patch_weight.shape[1]
    arrays = (
        slide_image, keep_flags, weight_one.transpose(0, 2, 1), offset_one[None],
        weight_two.transpose(0, 2, 1), offset_two[None], weight_three, offset_three[None],
    )
    own = patches // 2
    vmem = pl.BlockSpec(memory_space=pltpu.VMEM)
    anywhere = pl.BlockSpec(memory_space=pltpu.HBM)
    dma = pltpu.SemaphoreType.DMA
    dealt, pw = pl.pallas_call(
        functools.partial(kernel, n, n_seq, cap),
        name="stem_and_deal",
        out_shape=(
            pltpu.VMEM((own, width + 128), BF16),
            pltpu.VMEM(patch_weight.shape, BF16),
        ),
        in_specs=[pl.BlockSpec(memory_space=pltpu.SMEM)] + [anywhere] * 9,
        out_specs=(vmem, pl.BlockSpec(memory_space=pltpu.VMEM)),
        scratch_shapes=[
            *(pltpu.VMEM(x.shape, x.dtype) for x in arrays),
            pltpu.VMEM((3, 8, 1024), BF16),
            pltpu.VMEM((3, 32, 128), BF16),
            pltpu.VMEM((3, 8, 128), BF16),
            pltpu.VMEM((n,) + keep_flags.shape, jnp.int32),
            pltpu.VMEM((3, 3, 80, 128), F32),
            pltpu.VMEM((72, 1152), F32),
            pltpu.VMEM((1280, 128), F32),
            pltpu.VMEM((M1, 256), BF16),
            pltpu.VMEM((256, 768), BF16),
            pltpu.VMEM((10, 560, 128), F32),
            pltpu.VMEM((9, M2, 128), F32),
            pltpu.VMEM((2, 4, M3, 128), F32),
            pltpu.VMEM((2, n, cap, width), BF16),
            pltpu.VMEM((2, n, cap, width), BF16),
            dma((3,)), dma((3,)), dma((n,)), dma((n,)), dma((2, n)), dma((2, n)), dma((8,)), dma(()),
        ],
        compiler_params=pltpu.CompilerParams(
            collective_id=0, has_side_effects=True, vmem_limit_bytes=VMEM1
        ),
    )(
        owner_shift, *arrays, patch_weight,
    )
    placed = pl.pallas_call(
        project,
        name="project",
        out_shape=jax.ShapeDtypeStruct((own, embed), BF16),
        in_specs=[vmem] * 3,
        out_specs=vmem,
        compiler_params=pltpu.CompilerParams(vmem_limit_bytes=16 << 20),
    )(dealt, pw, patch_offset.reshape(-1, 128))
    return placed[None]


def solution(mesh):
    args = (P(None, "strip", "seq"), P("strip", "seq"), P("seq")) + (P(),) * 8
    return jax.shard_map(
        functools.partial(local, mesh.shape["strip"], mesh.shape["seq"]),
        mesh=mesh, in_specs=args, out_specs=P("seq", "strip", None), check_vma=False,
    )
```
